32 devices in a mesh: gx: 8 (over z, x), gy: 2 (over y), gz: 2 (over core).
Axes of the slice: x: 2, y: 2, z: 4, core: 2. Of those that a mesh axis runs over, the one named last changes fastest.
Arguments:
- patches: bfloat16 [8, 2, 3, 64, 64, 256], P(None, 'gy', None, 'gx', None, 'gz'), may hold values from -8 to 308
Outputs:
- smooth: float32 [3, 256, 64, 128], P(None, 'gx', 'gy', 'gz')
- confidence: float32 [256, 64, 128], P('gx', 'gy', 'gz')
The draws below stay inside these ranges and needn't reach their ends.
All inputs are finite; a program needn't handle non-finite values.
Results may differ from the reference program's by a relative error of at most 0.0013.
Values may be sent and summed in bfloat16 or wider, within the bound.
No kernel may reach another device: no remote copies, remote signals or barrier semaphores. Data moves between devices by JAX's collectives and lax.ppermute only.
A program may use at most 192 MiB of HBM per device.

```python
import jax
import jax.numpy as jnp
from jax import lax

P_SIZE = 64
C = 3
NPX = 8
NPY = 2
NPZ = 4


def draw_patches(key, part):
    dims_all = (NPX, NPY, C, P_SIZE, P_SIZE, NPZ, P_SIZE)
    first_key = jax.random.fold_in(jax.random.fold_in(key, 17), 0)
    values = jnp.clip(2.0 * jax.random.normal(first_key, dims_all, jnp.float32), -8.0, 8.0)
    return values.reshape(NPX, NPY, C, P_SIZE, P_SIZE, NPZ * P_SIZE).astype(jnp.bfloat16)


def setup_inputs(seed: int = 0) -> dict:
    key_list = jax.random.split(jax.random.key(seed), 2)
    return {
        "patches": draw_patches(jax.random.fold_in(key_list[1], 71), 0),
    }


def gaussian(offsets, length):
    centre = (length - 1) / 2.0
    spread = length / 8.0
    return jnp.exp(-(offsets - centre) ** 2 / (2.0 * spread * spread))


def place_halves(values, axis_k, axis_h):
    leading = lax.index_in_dim(values, 0, axis_h, keepdims=False)
    trailing = lax.index_in_dim(values, 1, axis_h, keepdims=False)
    step = leading.shape[axis_k] // max(leading.shape[axis_k], 1)
    lead_pad = [(0, 0)] * leading.ndim
    trail_pad = [(0, 0)] * leading.ndim
    lead_pad[axis_k] = (0, 1)
    trail_pad[axis_k] = (1, 0)
    return jnp.pad(leading, lead_pad) + jnp.pad(trailing, trail_pad) * step


def fold_inner(weighted, stride):
    count_a, count_b, classes, length, _, depth = weighted.shape
    count_c = depth // length
    folded = weighted.reshape(count_a, count_b, classes, length, length, count_c, 2, stride)
    folded = place_halves(folded, 5, 6)
    depth_cells = (count_c + 1) * stride
    folded = folded.reshape(count_a, count_b, classes, length, 2, stride, depth_cells)
    folded = place_halves(folded, 1, 4)
    wide_cells = (count_b + 1) * stride
    folded = folded.transpose(0, 2, 3, 1, 4, 5)
    return folded.reshape(count_a, classes, 2, stride, wide_cells, depth_cells)


def fold_outer(folded):
    count_a, classes, _, stride, wide_cells, depth_cells = folded.shape
    placed = place_halves(folded, 0, 2)
    return placed.transpose(1, 0, 2, 3, 4).reshape(classes, (count_a + 1) * stride, wide_cells, depth_cells)


def weight_line(begin_at, number, stride):
    cells = begin_at + jnp.arange(number, dtype=jnp.int32)
    cell_index = cells // stride
    near_offset = (cells - cell_index * stride).astype(jnp.float32)
    length = 2 * stride
    line = gaussian(near_offset, length)
    return line + jnp.where(cell_index >= 1, gaussian(near_offset + stride, length), 0.0)


def count_line(begin_at, number, extent):
    cells = begin_at + jnp.arange(number, dtype=jnp.int32)
    return 3.0 - (cells == 0).astype(jnp.float32) - (cells == extent - 1).astype(jnp.float32)


def box_sum(padded):
    summed = padded[:, :, :, :-2] + padded[:, :, :, 1:-1] + padded[:, :, :, 2:]
    summed = summed[:, :, :-2] + summed[:, :, 1:-1] + summed[:, :, 2:]
    return summed[:, :-2] + summed[:, 1:-1] + summed[:, 2:]


def reference(patches):
    pos_x, pos_y, classes, length, _, depth = patches.shape
    stride = length // 2
    pos_z = depth // length
    profile = gaussian(jnp.arange(length).astype(jnp.float32), length)
    factor = profile[:, None, None] * profile[None, :, None] * jnp.tile(profile, pos_z)[None, None, :]

    def one_row(row):
        weighted = row[None].astype(jnp.float32) * factor
        return fold_inner(weighted, stride)[0]

    rows = lax.map(one_row, patches)
    accumulated = fold_outer(rows)
    cells_x, cells_y, cells_z = pos_x * stride, pos_y * stride, pos_z * stride
    accumulated = accumulated[:, :cells_x, :cells_y, :cells_z]
    line_x = weight_line(0, cells_x, stride)
    line_y = weight_line(0, cells_y, stride)
    line_z = weight_line(0, cells_z, stride)
    weight_sum = line_x[:, None, None] * line_y[None, :, None] * line_z[None, None, :]
    logits = accumulated / weight_sum
    probability = jax.nn.softmax(logits, axis=0)
    padded = jnp.pad(probability, ((0, 0), (1, 1), (1, 1), (1, 1)))
    counts = count_line(0, cells_x, cells_x)[:, None, None] * count_line(0, cells_y, cells_y)[None, :, None]
    counts = counts * count_line(0, cells_z, cells_z)[None, None, :]
    smooth = box_sum(padded) / counts
    return smooth, jnp.max(smooth, axis=0)
```

```python
import functools

import jax
import jax.numpy as jnp
import numpy as np
from jax import lax
from jax.experimental import pallas as pl
from jax.experimental.pallas import tpu as pltpu
from jax.sharding import PartitionSpec as P


KNEE = 2.0
BASE = 2.0**-3.75
POWER = 32


def encode(d):
    t = jnp.abs(d) * (BASE / KNEE) + BASE
    for _ in range(5):
        t = t * t
    return jnp.where(d < 0.0, -t, t).astype(jnp.bfloat16)


def decode(code):
    v = code.astype(jnp.float32)
    t = jnp.exp(jnp.log(jnp.abs(v)) * (1.0 / POWER))
    d = t * (KNEE / BASE) - KNEE
    return jnp.where(v < 0.0, -d, d)


def shares(count, length):
    stride = length // 2
    u = np.arange(length, dtype=np.float64)
    g = np.exp(-((u - (length - 1) / 2.0) ** 2) / (2.0 * (length / 8.0) ** 2))
    pair = g[:stride] + g[stride:]
    table = np.tile(np.concatenate([g[:stride] / pair, g[stride:] / pair]), (count, 1))
    table[0, :stride] = 1.0
    return table.astype(np.float32)


def lane_index(shape):
    return lax.broadcasted_iota(jnp.int32, shape, len(shape) - 1)


def fold_kernel(dims, scal, own_ref, recv_ref, nx_ref, ny_ref, wz_ref, *refs):
    length, half, stride, first, far = (
        dims["length"], dims["half"], dims["stride"], dims["first"], dims["far"],
    )
    own_out, up_out, down_out, next_out = refs[:4]
    e_up, e_down, e_next = refs[4 + far : 7 + far]
    g, row, core = scal[0], scal[1], scal[2]
    target = g ^ (first + pl.program_id(0))
    begin = (g * 2 + core) * half
    upper = (begin >= stride).astype(jnp.int32)
    a = jnp.maximum(target - upper, 0)
    alive = (target >= upper).astype(jnp.float32)
    low = core == 0
    ny = ny_ref[row]
    for u in range(half):
        nx = nx_ref[a, begin + u] * alive
        w = [wz_ref[i] * nx for i in range(4)]
        own = [own_ref[0, 0, k, u].astype(jnp.float32) for k in range(3)]
        recv = [recv_ref[0, 0, k, u].astype(jnp.float32) for k in range(3)]
        for k in range(2):
            o, r = own[k + 1] - own[0], recv[k + 1] - recv[0]
            lo, hi = jnp.where(low, o, r), jnp.where(low, r, o)
            total = lo.reshape(-1, 8, 128) * w[0]
            total += pltpu.roll(lo, 128 - stride, 1).reshape(-1, 8, 128) * w[1]
            total += pltpu.roll(hi, 2 * stride, 1).reshape(-1, 8, 128) * w[2]
            total += pltpu.roll(hi, stride, 1).reshape(-1, 8, 128) * w[3]
            total = total.reshape(length, 128) * ny
            i = k * half + u
            own_out[0, i] = total[:stride]
            up_out[0, i * stride : (i + 1) * stride] = encode(total[stride:])
            e_up[i : i + 1] = total[stride - 1 : stride]
            e_down[i : i + 1] = total[:1]
            e_next[i : i + 1] = total[stride : stride + 1]
            if far:
                refs[7 + far][i : i + 1] = total[length - 1 :]
    main = 2 * half * stride
    up_out[0, main:] = encode(e_up[...])
    down_out[0] = encode(e_down[...])
    next_out[0] = e_next[...]
    if far:
        refs[4][0] = encode(refs[7 + far][...])


def join_kernel(dims, scal, own_ref, up_ref, down_ref, next_ref, *refs):
    half, stride, count, far, rows = (
        dims["half"], dims["stride"], dims["count"], dims["far"], dims["rows"],
    )
    outs = refs[far : far + count]
    buf, edge = refs[far + count :]
    row, rows_y = scal[1], dims["rows_y"]
    for j in range(2 * half):
        got = decode(up_ref[0, j * stride : (j + 1) * stride])
        total = own_ref[0, j] + jnp.where(row > 0, got, 0.0)
        buf[j * stride : (j + 1) * stride] = encode(total)
    lo = jnp.where(row > 0, decode(up_ref[0, 2 * half * stride :]), 0.0)
    if far:
        lo += jnp.where(row > 1, decode(refs[0][0]), 0.0)
    hi = next_ref[0] + jnp.where(row < rows_y - 1, decode(down_ref[0]), 0.0)
    edge[...] = jnp.zeros_like(edge)
    edge[: 2 * half] = lo[: 2 * half]
    edge[2 * half : 4 * half] = hi[: 2 * half]
    buf[2 * half * stride :] = encode(edge[...])
    for k in range(count):

        @pl.when(pl.program_id(0) == k)
        def _():
            outs[k][...] = buf[...]


def z_sum(p):
    lanes = lane_index(p.shape)
    before = jnp.where(lanes == 0, 0.0, pltpu.roll(p, 1, p.ndim - 1))
    after = jnp.where(lanes == 127, 0.0, pltpu.roll(p, 127, p.ndim - 1))
    return before + p + after


def two_classes(d1, d2):
    top = jnp.maximum(jnp.maximum(d1, d2), 0.0)
    e0, e1, e2 = jnp.exp(-top), jnp.exp(d1 - top), jnp.exp(d2 - top)
    inverse = 1.0 / (e0 + e1 + e2)
    return e0 * inverse, e1 * inverse


def smooth_kernel(dims, scal, *refs):
    half, stride, slabs, rows_y = dims["half"], dims["stride"], dims["slabs"], dims["rows_y"]
    codes, (keep, send, edge_same, edge_cross), pad = (
        refs[: 2 * slabs], refs[2 * slabs : 2 * slabs + 4], refs[2 * slabs + 4],
    )
    g, row, core = scal[0], scal[1], scal[2]
    low = core == 0
    main = 2 * half * stride
    left = lane_index((stride, 128)) < 64
    for s in range(slabs):
        t = (g & (slabs - 1)) ^ s

        def total(begin, size):
            part = slice(begin, begin + size)
            return decode(codes[s][part]) + decode(codes[s + slabs][part])

        d = total(main, dims["edge"])
        ends = two_classes(d, jnp.concatenate([d[half:], d[:half]], axis=0))
        ends = [z_sum(e) for e in ends]
        for u in range(half):
            d1 = total(u * stride, stride)
            d2 = total((half + u) * stride, stride)
            sums = []
            for k, p in enumerate(two_classes(d1, d2)):
                at = pad.at[u, k]
                at[8 : 8 + stride] = z_sum(p)
                at[7:8] = jnp.where(row > 0, ends[k][u : u + 1], 0.0)
                at[8 + stride : 9 + stride] = jnp.where(
                    row < rows_y - 1, ends[k][2 * half + u : 2 * half + u + 1], 0.0
                )
                sums.append(at[7 : 7 + stride] + at[8 : 8 + stride] + at[9 : 9 + stride])
            z0 = jnp.where(left, sums[0], pltpu.roll(sums[1], 64, 1))
            z1 = jnp.where(left, pltpu.roll(sums[0], 64, 1), sums[1])
            keep[t, u] = jnp.where(low, z0, z1)
            send[t, u] = jnp.where(low, z1, z0)
    at, u = jnp.where(low, 0, slabs - 1), jnp.where(low, 0, half - 1)
    edge_same[...] = keep[at, u]
    edge_cross[...] = send[at, u]


def finish_kernel(dims, scal, keep, recv, same, cross, smooth, confidence):
    half, stride, slabs, depth = dims["half"], dims["stride"], dims["slabs"], dims["depth"]
    g, row, core = scal[0], scal[1], scal[2]
    low = core == 0
    t = pl.program_id(0)

    def lower(at, u):
        return jnp.where(low, keep[at, u], recv[at, u])

    def higher(at, u):
        return jnp.where(low, recv[at, u], keep[at, u])

    first = jnp.where(low, cross[...], same[...])
    last = jnp.where(low, same[...], cross[...])
    before = jnp.where(t > 0, higher(jnp.maximum(t - 1, 0), half - 1), first)
    after = jnp.where(t < slabs - 1, lower(jnp.minimum(t + 1, slabs - 1), 0), last)
    lines = [before] + [lower(t, u) for u in range(half)]
    lines += [higher(t, u) for u in range(half)] + [after]
    shape = (stride, 128)
    y = row * stride + lax.broadcasted_iota(jnp.int32, shape, 0)
    z = core * depth + (lane_index(shape) & (depth - 1))

    def line_count(cell, extent):
        return 3.0 - (cell == 0).astype(jnp.float32) - (cell == extent - 1).astype(jnp.float32)

    counts = line_count(y, dims["rows_y"] * stride) * line_count(z, 2 * depth)
    for i in range(2 * half):
        x = g * stride + t * 2 * half + i
        total = lines[i] + lines[i + 1] + lines[i + 2]
        total = total / (counts * line_count(x, dims["extent_x"]))
        c0 = total[:, :depth]
        c1 = pltpu.roll(total, 64, 1)[:, :depth]
        c2 = jnp.maximum(1.0 - (c0 + c1), 0.0)
        smooth[0, i] = c0
        smooth[1, i] = c1
        smooth[2, i] = c2
        confidence[i] = jnp.maximum(jnp.maximum(c0, c1), c2)


def vmem(*shape):
    return pltpu.VMEM(shape, jnp.float32)


def whole(shape):
    return pl.BlockSpec(shape, lambda *_: (0,) * len(shape))


def per_device(patches):
    positions, per_y, classes, slab, length, lanes = patches.shape
    nx_dev, ny_dev, nz_dev = (lax.axis_size(n) for n in ("gx", "gy", "gz"))
    stride = length // 2
    half = slab // nz_dev
    assert positions == nx_dev and per_y == 1 and classes == 3 and nz_dev == 2
    assert lanes == 128 and length == 64
    slabs = nx_dev // 2
    depth = lanes // 2
    main, edge = 2 * half * stride, max(16, 4 * half)
    rows = main + edge
    far = int(ny_dev > 2)
    g, row, core = (lax.axis_index(n) for n in ("gx", "gy", "gz"))
    scal = jnp.stack([g, row, core]).astype(jnp.int32)
    dims = dict(
        length=length, half=half, stride=stride, slabs=slabs, rows=rows, edge=edge, far=far,
        rows_y=ny_dev, depth=depth, extent_x=positions * stride,
    )

    nx = jnp.asarray(shares(positions, length))
    ny = jnp.asarray(np.broadcast_to(shares(ny_dev, length)[:, :, None], (ny_dev, length, 128)))
    nz = shares(nz_dev * 2, length)
    z = np.zeros((4, 128), np.float32)
    for k in range(4):
        begin = k * stride
        size = min(length, 128 - begin)
        z[k, begin : begin + size] = nz[k, :size]
    wz = jnp.asarray(np.broadcast_to(z[:, None], (4, 8, 128)))

    upper = ((g * 2 + core) * half >= stride).astype(jnp.int32)

    def ship(array, axis, by):
        size = lax.axis_size(axis)
        pairs = [(i, i + by) for i in range(size) if 0 <= i + by < size]
        return lax.ppermute(array, axis, pairs)

    def messages(first, count):
        base = (g ^ first) & ~(count - 1)
        start = jnp.clip(base - upper, 0, positions - count)
        other = lax.dynamic_slice(
            patches, (start, 0, 0, (1 - core) * half, 0, 0), (count, 1, 3, half, length, 128)
        )
        recv = lax.ppermute(other, "gz", [(0, 1), (1, 0)])
        d = dict(dims, first=first, count=count)

        def patch_of(i, s):
            up = (s[0] * 2 + s[2]) * half >= stride
            return jnp.maximum((s[0] ^ (first + i)) - up.astype(jnp.int32), 0)

        def start_of(s):
            up = (s[0] * 2 + s[2]) * half >= stride
            at = ((s[0] ^ first) & ~(count - 1)) - up.astype(jnp.int32)
            return jnp.clip(at, 0, positions - count)

        block = (1, 1, 3, half, length, 128)

        def out(shape, dtype):
            shape = (count,) + shape
            spec = pl.BlockSpec((1,) + shape[1:], lambda i, s: (i,) + (0,) * (len(shape) - 1))
            return jax.ShapeDtypeStruct(shape, dtype), spec

        outs = [
            out((2 * half, stride, 128), jnp.float32),
            out((rows, 128), jnp.bfloat16),
            out((edge, 128), jnp.bfloat16),
            out((edge, 128), jnp.float32),
        ] + [out((edge, 128), jnp.bfloat16)] * far
        folded = pl.pallas_call(
            functools.partial(fold_kernel, d),
            out_shape=[o[0] for o in outs],
            grid_spec=pltpu.PrefetchScalarGridSpec(
                num_scalar_prefetch=1,
                grid=(count,),
                in_specs=[
                    pl.BlockSpec(block, lambda i, s: (patch_of(i, s), 0, 0, s[2], 0, 0)),
                    pl.BlockSpec(
                        block, lambda i, s: (patch_of(i, s) - start_of(s), 0, 0, 0, 0, 0)
                    ),
                    pl.BlockSpec(memory_space=pltpu.SMEM),
                    whole((ny_dev, length, 128)),
                    whole((4, 8, 128)),
                ],
                out_specs=[o[1] for o in outs],
                scratch_shapes=[vmem(edge, 128)] * (3 + far),
            ),
            name="fold",
        )(scal, patches, recv, nx, ny, wz)
        own, up, down, ahead = folded[:4]
        got = [own, ship(up, "gy", 1), ship(down, "gy", -1), ahead]
        got += [ship(f, "gy", 2) for f in folded[4:]]
        return pl.pallas_call(
            functools.partial(join_kernel, d),
            out_shape=[jax.ShapeDtypeStruct((rows, 128), jnp.bfloat16)] * count,
            grid_spec=pltpu.PrefetchScalarGridSpec(
                num_scalar_prefetch=1,
                grid=(count,),
                in_specs=[
                    pl.BlockSpec((1, 2 * half, stride, 128), lambda i, s: (i, 0, 0, 0)),
                    pl.BlockSpec((1, rows, 128), lambda i, s: (i, 0, 0)),
                    pl.BlockSpec((1, edge, 128), lambda i, s: (i, 0, 0)),
                    pl.BlockSpec((1, edge, 128), lambda i, s: (i, 0, 0)),
                ] + [pl.BlockSpec((1, edge, 128), lambda i, s: (i, 0, 0))] * far,
                out_specs=[whole((rows, 128))] * count,
                scratch_shapes=[pltpu.VMEM((rows, 128), jnp.bfloat16), vmem(edge, 128)],
            ),
            name="join",
        )(scal, *got)

    parts = messages(0, positions)
    codes = [parts[0]] + [
        lax.ppermute(parts[s], "gx", [(i, i ^ s) for i in range(nx_dev)])
        for s in range(1, nx_dev)
    ]

    half_rows = (slabs, half, stride, 128)
    keep, send, edge_same, edge_cross = pl.pallas_call(
        functools.partial(smooth_kernel, dims),
        out_shape=[jax.ShapeDtypeStruct(half_rows, jnp.float32)] * 2
        + [jax.ShapeDtypeStruct((stride, 128), jnp.float32)] * 2,
        grid_spec=pltpu.PrefetchScalarGridSpec(
            num_scalar_prefetch=1,
            grid=(1,),
            in_specs=[whole((rows, 128))] * nx_dev,
            out_specs=[whole(half_rows)] * 2 + [whole((stride, 128))] * 2,
            scratch_shapes=[vmem(half, 2, stride + 16, 128)],
        ),
        name="smooth",
    )(scal, *codes)

    recv = lax.ppermute(send, "gz", [(0, 1), (1, 0)])

    def neighbours(swap):
        up = [(2 * i + 1, 2 * (i + 1) + 1 - swap) for i in range(nx_dev - 1)]
        down = [(2 * i, 2 * (i - 1) + swap) for i in range(1, nx_dev)]
        return up + down

    same = lax.ppermute(edge_same, ("gx", "gz"), neighbours(0))
    cross = lax.ppermute(edge_cross, ("gx", "gz"), neighbours(1))

    return tuple(
        pl.pallas_call(
            functools.partial(finish_kernel, dims),
            out_shape=[
                jax.ShapeDtypeStruct((3, stride, stride, depth), jnp.float32),
                jax.ShapeDtypeStruct((stride, stride, depth), jnp.float32),
            ],
            grid_spec=pltpu.PrefetchScalarGridSpec(
                num_scalar_prefetch=1,
                grid=(slabs,),
                in_specs=[whole(half_rows)] * 2 + [whole((stride, 128))] * 2,
                out_specs=[
                    pl.BlockSpec((3, 2 * half, stride, depth), lambda i, s: (0, i, 0, 0)),
                    pl.BlockSpec((2 * half, stride, depth), lambda i, s: (i, 0, 0)),
                ],
            ),
            name="finish",
        )(scal, keep, recv, same, cross)
    )


def solution(mesh):
    in_specs = (P(None, "gy", None, "gx", None, "gz"),)
    out_specs = (P(None, "gx", "gy", "gz"), P("gx", "gy", "gz"))
    return jax.shard_map(
        per_device, mesh=mesh, in_specs=in_specs, out_specs=out_specs, check_vma=False
    )
```

```python
import functools

import jax
import jax.numpy as jnp
from jax import lax
from jax.experimental import pallas as pl
from jax.experimental.pallas import tpu as pltpu
from jax.sharding import PartitionSpec as P


KNEE = 0.5
BASE = 2.0**-5
POWER = 17
LOG2E = 1.4426950408889634


def encode(d):
    t = d * (BASE / KNEE) + jnp.where(d < 0.0, -BASE, BASE)
    p = t
    for _ in range(4):
        p = p * p
    return (p * t).astype(jnp.bfloat16)


def decode(code, scale=1.0):
    v = code.astype(jnp.float32)
    t = jnp.exp2(jnp.log(jnp.abs(v)) * (LOG2E / POWER))
    k = scale * (KNEE / BASE)
    return (t - BASE) * jnp.where(v < 0.0, -k, k)


def share(cell, length, paired):
    stride = length // 2
    centre, spread = (length - 1) / 2.0, length / 8.0
    other = jnp.where(cell < stride, cell + stride, cell - stride).astype(jnp.float32)
    mine = cell.astype(jnp.float32)
    ratio = ((mine - centre) ** 2 - (other - centre) ** 2) / (2.0 * spread * spread)
    alone = jnp.logical_and(cell < stride, jnp.logical_not(paired))
    return jnp.where(alone, 1.0, 1.0 / (1.0 + jnp.exp(ratio)))


def index(shape, axis):
    return lax.broadcasted_iota(jnp.int32, shape, axis)


def fold_kernel(dims, scal, own_ref, recv_ref, own_out, up_out, next_out, ny, wz, edge):
    length, half, stride, first, base = (
        dims["length"], dims["half"], dims["stride"], dims["first"], dims["base"],
    )
    g, row, core = scal[0], scal[1], scal[2]
    low = core == 0
    left = index((1, 128), 1) < 64

    @pl.when(pl.program_id(0) == 0)
    def _():
        cell = index((length, 128), 0)
        ny[...] = share(cell, length, jnp.full(cell.shape, row) > 0)
        lane = index((8, 128), 1)
        cell = lane & (length - 1)
        wz[0] = share(cell, length, lane >= length)
        odd = (lane - stride) & (length - 1)
        wz[1] = jnp.where(lane < stride, 0.0, share(odd, length, lane >= 0))
        edge[...] = jnp.zeros_like(edge)

    target = g ^ (first + pl.program_id(0))
    begin = (g * 2 + core) * half
    upper = (begin >= stride).astype(jnp.int32)
    a = target - upper
    recv_at = jnp.maximum(a, 0) - base(g, core)
    for u in range(half):
        cell = jnp.full((8, 128), begin + u)
        nx = share(cell, length, jnp.full(cell.shape, a) > 0)
        nx = jnp.where(jnp.full(cell.shape, a) >= 0, nx, 0.0)
        even, odd = wz[0] * nx, wz[1] * nx
        lo, hi = [], []
        for k in range(3):
            o, r = own_ref[0, 0, k, u], recv_ref[recv_at, 0, k, u]
            lo.append(jnp.where(low, o, r).astype(jnp.float32))
            hi.append(jnp.where(low, r, o).astype(jnp.float32))
        for k in range(2):
            a0, b0 = lo[k + 1] - lo[0], hi[k + 1] - hi[0]
            s = jnp.where(left, a0, pltpu.roll(b0, 64, 1))
            t = jnp.where(left, pltpu.roll(a0, 64, 1), b0)
            total = s.reshape(-1, 8, 128) * even
            total += pltpu.roll(t, stride, 1).reshape(-1, 8, 128) * odd
            total = total.reshape(length, 128) * ny[...]
            i = k * half + u
            own_out[0, i] = total[:stride]
            up_out[0, i * stride : (i + 1) * stride] = encode(total[stride:])
            for n, at in enumerate((stride - 1, 0, length - 1, stride)):
                edge[2 * half * n + i : 2 * half * n + i + 1] = total[at : at + 1]
    up_out[0, 2 * half * stride :] = encode(edge[...])
    next_out[0] = edge[6 * half : 8 * half]


def join_kernel(dims, scal, own_ref, next_ref, up_ref, down_ref, *refs):
    half, stride, count, edge_rows = dims["half"], dims["stride"], dims["count"], dims["edge"]
    far = refs[:-count]
    outs = refs[len(far) : len(far) + count]
    row, rows_y = scal[1], dims["rows_y"]
    from_below = (row > 0).astype(jnp.float32)
    from_above = (row < rows_y - 1).astype(jnp.float32)
    main, group = 2 * half * stride, 2 * half

    def body(j, carry):
        part = pl.ds(pl.multiple_of(j * stride, stride), stride)
        for k in range(count):
            outs[k][part] = encode(own_ref[k, j] + decode(up_ref[k, part], from_below))
        return carry

    lax.fori_loop(0, 2 * half, body, 0)
    for k in range(count):
        lo = decode(up_ref[k, main:], from_below)[:group]
        hi = next_ref[k] + decode(down_ref[k, main:], from_above)[group : 2 * group]
        for f in far:
            beyond = (row > 1).astype(jnp.float32)
            lo += decode(f[k, main:], beyond)[2 * group : 3 * group]
        both = jnp.concatenate([lo, hi], axis=0)
        both = jnp.concatenate([both] * (edge_rows // (2 * group)), axis=0)
        outs[k][main:] = encode(both)


def z_sum(p):
    lanes = index(p.shape, p.ndim - 1)
    before = jnp.where(lanes == 0, 0.0, pltpu.roll(p, 1, p.ndim - 1))
    after = jnp.where(lanes == 127, 0.0, pltpu.roll(p, 127, p.ndim - 1))
    return before + p + after


def two_classes(d1, d2):
    top = jnp.maximum(jnp.maximum(d1, d2), 0.0)
    e0, e1, e2 = jnp.exp(-top), jnp.exp(d1 - top), jnp.exp(d2 - top)
    inverse = 1.0 / (e0 + e1 + e2)
    return e0 * inverse, e1 * inverse


def ends_of(dims, scal, here, there, pad):
    half, stride = dims["half"], dims["stride"]
    main = slice(2 * half * stride, None)
    d = decode(here[main]) + decode(there[main])
    row = scal[1]
    for k, p in enumerate(two_classes(d, jnp.concatenate([d[half:], d[:half]], axis=0))):
        for u in range(half):
            lo, hi = p[u : u + 1], p[2 * half + u : 2 * half + u + 1]
            pad[u, k, 7:8] = jnp.where(row > 0, lo, 0.0)
            pad[u, k, 8 + stride : 9 + stride] = jnp.where(row < dims["rows_y"] - 1, hi, 0.0)


def halves_of(dims, here, there, u, pad):
    half, stride = dims["half"], dims["stride"]

    def total(j):
        part = pl.ds(pl.multiple_of(j * stride, stride), stride)
        return decode(here[part]) + decode(there[part])

    sums = []
    for k, p in enumerate(two_classes(total(u), total(half + u))):
        at = pad.at[u, k]
        at[8 : 8 + stride] = p
        sums.append(z_sum(at[7 : 7 + stride] + p + at[9 : 9 + stride]))
    left = index((stride, 128), 1) < 64
    return (
        jnp.where(left, sums[0], pltpu.roll(sums[1], 64, 1)),
        jnp.where(left, pltpu.roll(sums[0], 64, 1), sums[1]),
    )


def edge_kernel(dims, scal, *refs):
    half, slabs = dims["half"], dims["slabs"]
    codes, same, cross, pad = refs[: 2 * slabs], refs[-3], refs[-2], refs[-1]
    g, core = scal[0], scal[2]
    low = core == 0
    at = (g & (slabs - 1)) ^ jnp.where(low, 0, slabs - 1)
    u = jnp.where(low, 0, half - 1)
    for s in range(slabs):

        @pl.when(at == s)
        def _():
            ends_of(dims, scal, codes[s], codes[s + slabs], pad)
            z0, z1 = halves_of(dims, codes[s], codes[s + slabs], u, pad)
            same[...] = jnp.where(low, z0, z1)
            cross[...] = jnp.where(low, z1, z0)


def smooth_kernel(dims, scal, *refs):
    half, slabs = dims["half"], dims["slabs"]
    codes, keep, send, pad = refs[: 2 * slabs], refs[-3], refs[-2], refs[-1]
    g, core = scal[0], scal[2]
    low = core == 0
    for s in range(slabs):
        t = (g & (slabs - 1)) ^ s
        mine = pad.at[s]
        ends_of(dims, scal, codes[s], codes[s + slabs], mine)
        for u in range(half):
            z0, z1 = halves_of(dims, codes[s], codes[s + slabs], u, mine)
            keep[t, u] = jnp.where(low, z0, z1)
            send[t, u] = jnp.where(low, z1, z0)


def finish_kernel(dims, scal, keep, recv, same, cross, smooth, confidence):
    half, stride, slabs, depth = dims["half"], dims["stride"], dims["slabs"], dims["depth"]
    step = dims["step"]
    g, row, core = scal[0], scal[1], scal[2]
    low = core == 0
    t = pl.program_id(0) * step

    def lower(at, u):
        return jnp.where(low, keep[at, u], recv[at, u])

    def higher(at, u):
        return jnp.where(low, recv[at, u], keep[at, u])

    first = jnp.where(low, cross[...], same[...])
    last = jnp.where(low, same[...], cross[...])
    lines = [jnp.where(t > 0, higher(jnp.maximum(t - 1, 0), half - 1), first)]
    for i in range(step):
        lines += [lower(t + i, u) for u in range(half)]
        lines += [higher(t + i, u) for u in range(half)]
    end = t + step
    lines += [jnp.where(end < slabs, lower(jnp.minimum(end, slabs - 1), 0), last)]
    shape = (stride, 128)
    y = row * stride + index(shape, 0)
    z = core * depth + (index(shape, 1) & (depth - 1))

    def line_count(cell, extent):
        return 3.0 - (cell == 0).astype(jnp.float32) - (cell == extent - 1).astype(jnp.float32)

    inverse = 1.0 / (line_count(y, dims["rows_y"] * stride) * line_count(z, 2 * depth))
    for i in range(2 * half * step):
        x = jnp.full((8, 128), g * stride + t * 2 * half + i)
        scale = 1.0 / line_count(x, dims["extent_x"])
        total = (lines[i] + lines[i + 1] + lines[i + 2]) * inverse
        total = (total.reshape(-1, 8, 128) * scale).reshape(shape)
        c0 = total[:, :depth]
        c1 = pltpu.roll(total, 64, 1)[:, :depth]
        c2 = jnp.maximum(1.0 - (c0 + c1), 0.0)
        smooth[0, i] = c0
        smooth[1, i] = c1
        smooth[2, i] = c2
        confidence[i] = jnp.maximum(jnp.maximum(c0, c1), c2)


def vmem(*shape):
    return pltpu.VMEM(shape, jnp.float32)


def whole(shape):
    return pl.BlockSpec(shape, lambda *_: (0,) * len(shape))


def like(shape, dtype=jnp.float32):
    return jax.ShapeDtypeStruct(shape, dtype)


def call(kernel, name, scal, args, outs, in_specs=None, out_specs=None, grid=(1,), scratch=(),
         mib=4, flops=0):
    args = list(args)
    size = sum(a.size * a.dtype.itemsize for a in args + list(outs))
    return pl.pallas_call(
        kernel,
        out_shape=list(outs),
        grid_spec=pltpu.PrefetchScalarGridSpec(
            num_scalar_prefetch=1,
            grid=grid,
            in_specs=in_specs or [whole(a.shape) for a in args],
            out_specs=out_specs or [whole(o.shape) for o in outs],
            scratch_shapes=list(scratch),
        ),
        compiler_params=pltpu.CompilerParams(vmem_limit_bytes=mib << 20),
        cost_estimate=pl.CostEstimate(flops=flops, bytes_accessed=size, transcendentals=0),
        name=name,
    )(scal, *args)


def per_device(patches):
    positions, per_y, classes, slab, length, lanes = patches.shape
    nx_dev, ny_dev, nz_dev = (lax.axis_size(n) for n in ("gx", "gy", "gz"))
    stride = length // 2
    half = slab // nz_dev
    assert positions == nx_dev and per_y == 1 and classes == 3 and nz_dev == 2
    assert lanes == 128 and length == 64
    slabs = nx_dev // 2
    depth = lanes // 2
    main, edge = 2 * half * stride, 8 * half
    rows = main + edge
    far = int(ny_dev > 2)
    g, row, core = (lax.axis_index(n) for n in ("gx", "gy", "gz"))
    scal = jnp.stack([g, row, core]).astype(jnp.int32)
    dims = dict(
        length=length, half=half, stride=stride, slabs=slabs, rows=rows, edge=edge, far=far,
        rows_y=ny_dev, depth=depth, extent_x=positions * stride,
    )

    def ship(array, axis, by):
        size = lax.axis_size(axis)
        pairs = [(i, i + by) for i in range(size) if 0 <= i + by < size]
        return lax.ppermute(array, axis, pairs)

    def messages(first, count):
        def upper(g, core):
            return ((g * 2 + core) * half >= stride).astype(jnp.int32)

        def base(g, core):
            return jnp.clip(((g ^ first) & ~(count - 1)) - upper(g, core), 0, positions - count)

        def patch_of(i, s):
            return jnp.maximum((s[0] ^ (first + i)) - upper(s[0], s[2]), 0)

        other = lax.dynamic_slice(
            patches,
            (base(g, core), 0, 0, (1 - core) * half, 0, 0),
            (count, 1, 3, half, length, 128),
        )
        recv = lax.ppermute(other, "gz", [(0, 1), (1, 0)])
        d = dict(dims, first=first, count=count, base=base)
        block = (1, 1, 3, half, length, 128)
        outs = [
            like((count, 2 * half, stride, 128)),
            like((count, rows, 128), jnp.bfloat16),
            like((count, 2 * half, 128)),
        ]
        own, up, ahead = call(
            functools.partial(fold_kernel, d), "fold", scal, [patches, recv], outs,
            in_specs=[
                pl.BlockSpec(block, lambda i, s: (patch_of(i, s), 0, 0, s[2], 0, 0)),
                whole(recv.shape),
            ],
            out_specs=[
                pl.BlockSpec((1,) + o.shape[1:], lambda i, s, o=o: (i,) + (0,) * (len(o.shape) - 1))
                for o in outs
            ],
            grid=(count,),
            scratch=[vmem(length, 128), vmem(2, 8, 128), vmem(edge, 128)],
        )
        if ny_dev == 2:
            below = above = lax.ppermute(up, "gy", [(0, 1), (1, 0)])
        else:
            below, above = ship(up, "gy", 1), ship(up, "gy", -1)
        beyond = [ship(up, "gy", 2)] * far
        return call(
            functools.partial(join_kernel, d), "join", scal,
            [own, ahead, below, above] + beyond,
            [like((rows, 128), jnp.bfloat16)] * count,
        )

    def exchange(part, s):
        return lax.ppermute(part, "gx", [(i, i ^ s) for i in range(nx_dev)]) if s else part

    late = messages(slabs, slabs)
    soon = messages(0, slabs)
    codes = [exchange(p, s) for s, p in enumerate(list(soon) + list(late))]

    half_rows = (slabs, half, stride, 128)
    row_like = like((stride, 128))
    edge_same, edge_cross = call(
        functools.partial(edge_kernel, dims), "edges", scal, codes, [row_like] * 2,
        scratch=[vmem(half, 2, stride + 16, 128)],
    )

    def neighbours(swap):
        up = [(2 * i + 1, 2 * (i + 1) + 1 - swap) for i in range(nx_dev - 1)]
        down = [(2 * i, 2 * (i - 1) + swap) for i in range(1, nx_dev)]
        return up + down

    same = lax.ppermute(edge_same, ("gx", "gz"), neighbours(0))
    cross = lax.ppermute(edge_cross, ("gx", "gz"), neighbours(1))
    keep, send = call(
        functools.partial(smooth_kernel, dims), "smooth", scal, codes, [like(half_rows)] * 2,
        scratch=[vmem(slabs, half, 2, stride + 16, 128)],
    )
    recv = lax.ppermute(send, "gz", [(0, 1), (1, 0)])

    step = slabs // 2
    return tuple(
        call(
            functools.partial(finish_kernel, dict(dims, step=step)), "finish", scal,
            [keep, recv, same, cross],
            [like((3, stride, stride, depth)), like((stride, stride, depth))],
            out_specs=[
                pl.BlockSpec((3, 2 * half * step, stride, depth), lambda i, s: (0, i, 0, 0)),
                pl.BlockSpec((2 * half * step, stride, depth), lambda i, s: (i, 0, 0)),
            ],
            grid=(slabs // step,),
            mib=8,
        )
    )


def solution(mesh):
    in_specs = (P(None, "gy", None, "gx", None, "gz"),)
    out_specs = (P(None, "gx", "gy", "gz"), P("gx", "gy", "gz"))
    return jax.shard_map(
        per_device, mesh=mesh, in_specs=in_specs, out_specs=out_specs, check_vma=False
    )
```

```python
import functools

import jax
import jax.numpy as jnp
import numpy as np
from jax import lax
from jax.experimental import pallas as pl
from jax.experimental.pallas import tpu as pltpu
from jax.sharding import PartitionSpec as P


KNEE = 0.5
BASE = 2.0**-5
POWER = 17
LOG2E = 1.4426950408889634


def encode(d):
    t = d * (BASE / KNEE) + jnp.where(d < 0.0, -BASE, BASE)
    p = t
    for _ in range(4):
        p = p * p
    return (p * t).astype(jnp.bfloat16)


def decode(code, scale=1.0):
    v = code.astype(jnp.float32)
    t = jnp.exp2(jnp.log(jnp.abs(v)) * (LOG2E / POWER))
    k = scale * (KNEE / BASE)
    return (t - BASE) * jnp.where(v < 0.0, -k, k)


def share(cell, length, paired):
    stride = length // 2
    centre, spread = (length - 1) / 2.0, length / 8.0
    other = jnp.where(cell < stride, cell + stride, cell - stride).astype(jnp.float32)
    mine = cell.astype(jnp.float32)
    ratio = ((mine - centre) ** 2 - (other - centre) ** 2) / (2.0 * spread * spread)
    alone = jnp.logical_and(cell < stride, jnp.logical_not(paired))
    return jnp.where(alone, 1.0, 1.0 / (1.0 + jnp.exp(ratio)))


def z_weights(length, depth):
    stride, count = length // 2, 2 * depth // (length // 2)
    u = np.arange(length, dtype=np.float64)
    g = np.exp(-((u - (length - 1) / 2.0) ** 2) / (2.0 * (length / 8.0) ** 2))
    table = np.zeros((count * length, 2 * depth), np.float32)
    for k in range(count):
        for w in range(length):
            z = k * stride + w
            if z < 2 * depth:
                alone = k == 0 and w < stride
                pair = 0.0 if alone else g[w + stride if w < stride else w - stride]
                table[k * length + w, z] = g[w] / (g[w] + pair)
    high = table.astype(jnp.bfloat16)
    low = (table - high.astype(np.float32)).astype(jnp.bfloat16)
    both = np.concatenate([high, low], 1)
    return np.stack([both, np.roll(both, count * length // 2, 0)])


def index(shape, axis):
    return lax.broadcasted_iota(jnp.int32, shape, axis)


def pick_kernel(dims, scal, patches, out, sem):
    count, half = dims["count"], dims["half"]
    start = dims["base"](scal[0], scal[2])
    rows = pl.ds((1 - scal[2]) * half, half)
    copy = pltpu.make_async_copy(patches.at[pl.ds(start, count), :, :, rows], out, sem)
    copy.start()
    copy.wait()


def fold_kernel(dims, scal, own_ref, recv_ref, w_ref, own_out, up_out, next_out, ny, edge):
    length, half, stride, first = dims["length"], dims["half"], dims["stride"], dims["first"]
    g, row, core = scal[0], scal[1], scal[2]
    begin = (g * 2 + core) * half
    upper = (begin >= stride).astype(jnp.int32)
    cell = index((length, 128), 0)
    ny[...] = share(cell, length, jnp.full(cell.shape, row) > 0)
    edge[...] = jnp.zeros_like(edge)
    shape = (8, 128)
    nx_pair = [
        share(jnp.full(shape, begin + u), length, jnp.full(shape, 1) > 0) for u in range(half)
    ]
    weights = w_ref[core]

    def body(i, carry):
        a = (g ^ (first + i)) - upper
        at = jnp.maximum(a, 0)
        recv_at = at - dims["base"](g, core)
        for u in range(half):
            nx = jnp.where(jnp.logical_and(a == 0, upper == 0), 1.0, nx_pair[u])
            nx = jnp.where(a < 0, 0.0, nx)
            both = (ny[...].reshape(-1, 8, 128) * nx).reshape(length, 128)
            rows = [
                jnp.concatenate([own_ref[at, 0, k, core * half + u], recv_ref[recv_at, 0, k, u]], 1)
                for k in range(3)
            ]
            part = jnp.dot(
                jnp.concatenate(rows, 0), weights, preferred_element_type=jnp.float32
            )
            part = part[:, :128] + part[:, 128:]
            for k in range(2):
                total = (part[(k + 1) * length : (k + 2) * length] - part[:length]) * both
                j = k * half + u
                own_out[i, j] = total[:stride]
                up_out[i, j * stride : (j + 1) * stride] = encode(total[stride:])
                for n, line in enumerate(dims["lines"]):
                    edge[2 * half * n + j : 2 * half * n + j + 1] = total[line : line + 1]
                next_out[i, j : j + 1] = total[stride : stride + 1]
        up_out[i, 2 * half * stride :] = encode(edge[...])
        return carry

    lax.fori_loop(0, dims["count"], body, 0, unroll=2)


def join_kernel(dims, scal, own_ref, next_ref, up_ref, down_ref, *refs):
    half, stride, count, edge_rows = dims["half"], dims["stride"], dims["count"], dims["edge"]
    far = refs[:-count]
    outs = refs[len(far) : len(far) + count]
    row, rows_y = scal[1], dims["rows_y"]
    from_below = (row > 0).astype(jnp.float32)
    from_above = (row < rows_y - 1).astype(jnp.float32)
    main, group = 2 * half * stride, 2 * half

    def body(j, carry):
        part = pl.ds(pl.multiple_of(j * stride, stride), stride)
        for k in range(count):
            outs[k][part] = encode(own_ref[k, j] + decode(up_ref[k, part], from_below))
        return carry

    lax.fori_loop(0, 2 * half, body, 0)
    for k in range(count):
        lo = decode(up_ref[k, main:], from_below)[:group]
        hi = next_ref[k] + decode(down_ref[k, main:], from_above)[group : 2 * group]
        for f in far:
            beyond = (row > 1).astype(jnp.float32)
            lo += decode(f[k, main:], beyond)[2 * group : 3 * group]
        both = jnp.concatenate([lo, hi], axis=0)
        if edge_rows > 2 * group:
            both = jnp.concatenate([both] * (edge_rows // (2 * group)), axis=0)
        outs[k][main:] = encode(both)


def z_sum(p):
    lanes = index(p.shape, p.ndim - 1)
    before = jnp.where(lanes == 0, 0.0, pltpu.roll(p, 1, p.ndim - 1))
    after = jnp.where(lanes == 127, 0.0, pltpu.roll(p, 127, p.ndim - 1))
    return before + p + after


def two_classes(d1, d2):
    top = jnp.maximum(jnp.maximum(d1, d2), 0.0)
    e0, e1, e2 = jnp.exp2(-top), jnp.exp2(d1 - top), jnp.exp2(d2 - top)
    inverse = 1.0 / (e0 + e1 + e2)
    return e0 * inverse, e1 * inverse


def ends_of(dims, scal, here, there, pad):
    half, stride = dims["half"], dims["stride"]
    main = slice(2 * half * stride, None)
    d = decode(here[main], LOG2E) + decode(there[main], LOG2E)
    row = scal[1]
    for k, p in enumerate(two_classes(d, jnp.concatenate([d[half:], d[:half]], axis=0))):
        for u in range(half):
            lo, hi = p[u : u + 1], p[2 * half + u : 2 * half + u + 1]
            pad[u, k, 7:8] = jnp.where(row > 0, lo, 0.0)
            pad[u, k, 8 + stride : 9 + stride] = jnp.where(row < dims["rows_y"] - 1, hi, 0.0)


def halves_of(dims, here, there, u, pad):
    half, stride = dims["half"], dims["stride"]

    def total(j):
        part = pl.ds(pl.multiple_of(j * stride, stride), stride)
        return decode(here[part], LOG2E) + decode(there[part], LOG2E)

    sums = []
    for k, p in enumerate(two_classes(total(u), total(half + u))):
        at = pad.at[u, k]
        at[8 : 8 + stride] = p
        sums.append(z_sum(at[7 : 7 + stride] + p + at[9 : 9 + stride]))
    left = index((stride, 128), 1) < 64
    return (
        jnp.where(left, sums[0], pltpu.roll(sums[1], 64, 1)),
        jnp.where(left, pltpu.roll(sums[0], 64, 1), sums[1]),
    )


def edge_kernel(dims, scal, *refs):
    half, slabs = dims["half"], dims["slabs"]
    codes, ends, pad = refs[: 2 * slabs], refs[-2], refs[-1]
    g, core = scal[0], scal[2]
    low = core == 0
    at = (g & (slabs - 1)) ^ jnp.where(low, 0, slabs - 1)
    u = jnp.where(low, 0, half - 1)
    for s in range(slabs):

        @pl.when(at == s)
        def _():
            ends_of(dims, scal, codes[s], codes[s + slabs], pad)
            z0, z1 = halves_of(dims, codes[s], codes[s + slabs], u, pad)
            ends[0] = z0
            ends[1] = z1


def smooth_kernel(dims, scal, *refs):
    half, slabs = dims["half"], dims["slabs"]
    codes, keep, send, pad = refs[: 2 * slabs], refs[-3], refs[-2], refs[-1]
    g, core = scal[0], scal[2]
    low = core == 0
    for s in range(slabs):
        t = (g & (slabs - 1)) ^ s
        mine = pad.at[s]
        ends_of(dims, scal, codes[s], codes[s + slabs], mine)
        for u in range(half):
            z0, z1 = halves_of(dims, codes[s], codes[s + slabs], u, mine)
            keep[t, u] = jnp.where(low, z0, z1)
            send[t, u] = jnp.where(low, z1, z0)


def finish_kernel(dims, scal, keep, recv, mine, theirs, smooth, confidence):
    half, stride, slabs, depth = dims["half"], dims["stride"], dims["slabs"], dims["depth"]
    step = dims["step"]
    g, row, core = scal[0], scal[1], scal[2]
    low = core == 0
    t = pl.program_id(0) * step

    def lower(at, u):
        return jnp.where(low, keep[at, u], recv[at, u])

    def higher(at, u):
        return jnp.where(low, recv[at, u], keep[at, u])

    first = jnp.where(low, theirs[core], mine[core])
    last = jnp.where(low, mine[core], theirs[core])
    lines = [jnp.where(t > 0, higher(jnp.maximum(t - 1, 0), half - 1), first)]
    for i in range(step):
        lines += [lower(t + i, u) for u in range(half)]
        lines += [higher(t + i, u) for u in range(half)]
    end = t + step
    lines += [jnp.where(end < slabs, lower(jnp.minimum(end, slabs - 1), 0), last)]
    shape = (stride, 128)
    y = row * stride + index(shape, 0)
    z = core * depth + (index(shape, 1) & (depth - 1))

    def line_count(cell, extent):
        return 3.0 - (cell == 0).astype(jnp.float32) - (cell == extent - 1).astype(jnp.float32)

    inverse = 1.0 / (line_count(y, dims["rows_y"] * stride) * line_count(z, 2 * depth))
    for i in range(2 * half * step):
        x = jnp.full((8, 128), g * stride + t * 2 * half + i)
        scale = 1.0 / line_count(x, dims["extent_x"])
        total = (lines[i] + lines[i + 1] + lines[i + 2]) * inverse
        total = (total.reshape(-1, 8, 128) * scale).reshape(shape)
        c0 = total[:, :depth]
        c1 = pltpu.roll(total, 64, 1)[:, :depth]
        c2 = jnp.maximum(1.0 - (c0 + c1), 0.0)
        smooth[0, i] = c0
        smooth[1, i] = c1
        smooth[2, i] = c2
        confidence[i] = jnp.maximum(jnp.maximum(c0, c1), c2)


def vmem(*shape):
    return pltpu.VMEM(shape, jnp.float32)


def whole(shape):
    return pl.BlockSpec(shape, lambda *_: (0,) * len(shape))


def like(shape, dtype=jnp.float32):
    return jax.ShapeDtypeStruct(shape, dtype)


def call(kernel, scal, args, outs, in_specs=None, out_specs=None, grid=(1,), scratch=(),
         mib=4, flops=0):
    args = list(args)
    size = sum(a.size * a.dtype.itemsize for a in args + list(outs))
    return pl.pallas_call(
        kernel,
        out_shape=list(outs),
        grid_spec=pltpu.PrefetchScalarGridSpec(
            num_scalar_prefetch=1,
            grid=grid,
            in_specs=in_specs or [whole(a.shape) for a in args],
            out_specs=out_specs or [whole(o.shape) for o in outs],
            scratch_shapes=list(scratch),
        ),
        compiler_params=pltpu.CompilerParams(vmem_limit_bytes=int(mib * 2**20)),
        cost_estimate=pl.CostEstimate(flops=flops, bytes_accessed=size, transcendentals=0),
    )(scal, *args)


def stitched(patches):
    positions, per_y, classes, slab, length, lanes = patches.shape
    nx_dev, ny_dev, nz_dev = (lax.axis_size(n) for n in ("gx", "gy", "gz"))
    stride = length // 2
    half = slab // nz_dev
    assert positions == nx_dev and per_y == 1 and classes == 3 and nz_dev == 2
    assert lanes == 128 and length == 64
    slabs = nx_dev // 2
    depth = lanes // 2
    far = int(ny_dev > 2)
    edge, edge_y = (-(-n * 2 * half // 16) * 16 for n in (2, 2 + far))
    main = 2 * half * stride
    rows, rows_up = main + edge, main + edge_y
    g, row, core = (lax.axis_index(n) for n in ("gx", "gy", "gz"))
    scal = jnp.stack([g, row, core]).astype(jnp.int32)
    dims = dict(
        length=length, half=half, stride=stride, slabs=slabs, rows=rows, edge=edge, far=far,
        rows_y=ny_dev, depth=depth, extent_x=positions * stride,
        lines=(stride - 1, 0) + (length - 1,) * far,
    )
    weights = jnp.asarray(z_weights(length, depth))

    def ship(array, axis, by):
        size = lax.axis_size(axis)
        pairs = [(i, i + by) for i in range(size) if 0 <= i + by < size]
        return lax.ppermute(array, axis, pairs)

    def upper(g, core):
        return ((g * 2 + core) * half >= stride).astype(jnp.int32)

    def swapped(first, mib):
        def base(g, core):
            start = ((g ^ first) & ~(slabs - 1)) - upper(g, core)
            return jnp.clip(start, 0, positions - slabs)

        (other,) = call(
            functools.partial(pick_kernel, dict(dims, count=slabs, base=base)), scal,
            [patches], [like((slabs, 1, 3, half, length, 128), jnp.bfloat16)],
            in_specs=[pl.BlockSpec(memory_space=pl.ANY)],
            scratch=[pltpu.SemaphoreType.DMA(())],
            mib=mib,
        )
        return lax.ppermute(other, "gz", [(0, 1), (1, 0)]), base

    def messages(first, count, recv, base):
        d = dict(dims, first=first, count=count, base=base)
        own, up, ahead = call(
            functools.partial(fold_kernel, d), scal, [patches, recv, weights],
            [
                like((count, 2 * half, stride, 128)),
                like((count, rows_up, 128), jnp.bfloat16),
                like((count, 2 * half, 128)),
            ],
            scratch=[vmem(length, 128), vmem(edge_y, 128)],
        )
        if ny_dev == 2:
            below = above = lax.ppermute(up, "gy", [(0, 1), (1, 0)])
        else:
            below, above = ship(up, "gy", 1), ship(up, "gy", -1)
        beyond = [ship(up, "gy", 2)] * far
        parts = call(
            functools.partial(join_kernel, d), scal,
            [own, ahead, below, above] + beyond,
            [like((rows, 128), jnp.bfloat16)] * count,
        )
        return [
            lax.ppermute(p, "gx", [(i, i ^ s) for i in range(nx_dev)]) if s else p
            for s, p in enumerate(parts, first)
        ]

    recv_far = swapped(slabs, 61.5)
    recv_near = swapped(0, 4)
    first = messages(slabs, slabs // 2, *recv_far)
    second = messages(slabs + slabs // 2, slabs // 2, *recv_far)
    third = messages(0, slabs, *recv_near)
    codes = third + first + second

    half_rows = (slabs, half, stride, 128)
    (ends,) = call(
        functools.partial(edge_kernel, dims), scal, codes, [like((2, stride, 128))],
        scratch=[vmem(half, 2, stride + 16, 128)],
    )
    above = [(2 * i + 1, 2 * i + 3) for i in range(nx_dev - 1)]
    below = [(2 * i + 2, 2 * i) for i in range(nx_dev - 1)]
    mine = lax.ppermute(ends, ("gx", "gz"), above + below)
    codes, _ = lax.optimization_barrier((codes, ends))
    keep, send = call(
        functools.partial(smooth_kernel, dims), scal, codes, [like(half_rows)] * 2,
        scratch=[vmem(slabs, half, 2, stride + 16, 128)],
    )
    recv = lax.ppermute(send, "gz", [(0, 1), (1, 0)])
    theirs = lax.ppermute(mine, "gz", [(0, 1), (1, 0)])

    step = slabs // 2
    return tuple(
        call(
            functools.partial(finish_kernel, dict(dims, step=step)), scal,
            [keep, recv, mine, theirs],
            [like((3, stride, stride, depth)), like((stride, stride, depth))],
            out_specs=[
                pl.BlockSpec((3, 2 * half * step, stride, depth), lambda i, s: (0, i, 0, 0)),
                pl.BlockSpec((2 * half * step, stride, depth), lambda i, s: (i, 0, 0)),
            ],
            grid=(slabs // step,),
            mib=8,
        )
    )


def solution(mesh):
    in_specs = (P(None, "gy", None, "gx", None, "gz"),)
    out_specs = (P(None, "gx", "gy", "gz"), P("gx", "gy", "gz"))
    return jax.shard_map(
        stitched, mesh=mesh, in_specs=in_specs, out_specs=out_specs, check_vma=False
    )
```

```python
import functools

import jax
import jax.numpy as jnp
import numpy as np
from jax import lax
from jax.experimental import pallas as pl
from jax.experimental.pallas import tpu as pltpu
from jax.sharding import PartitionSpec as P


KNEE = 0.5
BASE = 2.0**-5
POWER = 17
LOG2E = 1.4426950408889634


def encode(d):
    t = d * (BASE / KNEE) + jnp.where(d < 0.0, -BASE, BASE)
    p = t
    for _ in range(4):
        p = p * p
    return (p * t).astype(jnp.bfloat16)


def decode(code, scale=1.0):
    v = code.astype(jnp.float32)
    t = jnp.exp2(jnp.log(jnp.abs(v)) * (LOG2E / POWER))
    k = scale * (KNEE / BASE)
    return (t - BASE) * jnp.where(v < 0.0, -k, k)


def share(cell, length, paired):
    stride = length // 2
    centre, spread = (length - 1) / 2.0, length / 8.0
    other = jnp.where(cell < stride, cell + stride, cell - stride).astype(jnp.float32)
    mine = cell.astype(jnp.float32)
    ratio = ((mine - centre) ** 2 - (other - centre) ** 2) / (2.0 * spread * spread)
    alone = jnp.logical_and(cell < stride, jnp.logical_not(paired))
    return jnp.where(alone, 1.0, 1.0 / (1.0 + jnp.exp(ratio)))


def z_weights(length, depth):
    stride, count = length // 2, 2 * depth // (length // 2)
    u = np.arange(length, dtype=np.float64)
    g = np.exp(-((u - (length - 1) / 2.0) ** 2) / (2.0 * (length / 8.0) ** 2))
    table = np.zeros((count * length, 2 * depth), np.float32)
    for k in range(count):
        for w in range(length):
            z = k * stride + w
            if z < 2 * depth:
                alone = k == 0 and w < stride
                pair = 0.0 if alone else g[w + stride if w < stride else w - stride]
                table[k * length + w, z] = g[w] / (g[w] + pair)
    high = table.astype(jnp.bfloat16)
    low = (table - high.astype(np.float32)).astype(jnp.bfloat16)
    both = np.concatenate([high, low], 1)
    return np.stack([both, np.roll(both, count * length // 2, 0)])


def index(shape, axis):
    return lax.broadcasted_iota(jnp.int32, shape, axis)


def pick_kernel(dims, scal, patches, out, sem):
    count, half = dims["count"], dims["half"]
    start = dims["base"](scal[0], scal[2])
    rows = pl.ds((1 - scal[2]) * half, half)
    copy = pltpu.make_async_copy(patches.at[pl.ds(start, count), :, :, rows], out, sem)
    copy.start()
    copy.wait()


def fold_kernel(dims, scal, own_ref, recv_ref, w_ref, own_out, up_out, next_out, ny, edge):
    length, half, stride, first = dims["length"], dims["half"], dims["stride"], dims["first"]
    g, row, core = scal[0], scal[1], scal[2]
    begin = (g * 2 + core) * half
    upper = (begin >= stride).astype(jnp.int32)
    cell = index((length, 128), 0)
    ny[...] = share(cell, length, jnp.full(cell.shape, row) > 0)
    edge[...] = jnp.zeros_like(edge)
    shape = (8, 128)
    nx_pair = [
        share(jnp.full(shape, begin + u), length, jnp.full(shape, 1) > 0) for u in range(half)
    ]
    weights = w_ref[core]

    def body(i, carry):
        a = (g ^ (first + i)) - upper
        at = jnp.maximum(a, 0)
        recv_at = at - dims["base"](g, core)
        for u in range(half):
            nx = jnp.where(jnp.logical_and(a == 0, upper == 0), 1.0, nx_pair[u])
            nx = jnp.where(a < 0, 0.0, nx)
            both = (ny[...].reshape(-1, 8, 128) * nx).reshape(length, 128)
            rows = [
                jnp.concatenate([own_ref[at, 0, k, core * half + u], recv_ref[recv_at, 0, k, u]], 1)
                for k in range(3)
            ]
            part = jnp.dot(
                jnp.concatenate(rows, 0), weights, preferred_element_type=jnp.float32
            )
            part = part[:, :128] + part[:, 128:]
            for k in range(2):
                total = (part[(k + 1) * length : (k + 2) * length] - part[:length]) * both
                j = k * half + u
                own_out[i, j] = total[:stride]
                up_out[i, j * stride : (j + 1) * stride] = encode(total[stride:])
                for n, line in enumerate(dims["lines"]):
                    edge[2 * half * n + j : 2 * half * n + j + 1] = total[line : line + 1]
                next_out[i, j : j + 1] = total[stride : stride + 1]
        up_out[i, 2 * half * stride :] = encode(edge[...])
        return carry

    lax.fori_loop(0, dims["count"], body, 0, unroll=2)


def join_kernel(dims, scal, own_ref, next_ref, up_ref, down_ref, *refs):
    half, stride, count, edge_rows = dims["half"], dims["stride"], dims["count"], dims["edge"]
    far = refs[:-count]
    outs = refs[len(far) : len(far) + count]
    row, rows_y = scal[1], dims["rows_y"]
    from_below = (row > 0).astype(jnp.float32)
    from_above = (row < rows_y - 1).astype(jnp.float32)
    main, group = 2 * half * stride, 2 * half

    def body(j, carry):
        part = pl.ds(pl.multiple_of(j * stride, stride), stride)
        for k in range(count):
            outs[k][part] = encode(own_ref[k, j] + decode(up_ref[k, part], from_below))
        return carry

    lax.fori_loop(0, 2 * half, body, 0)
    for k in range(count):
        lo = decode(up_ref[k, main:], from_below)[:group]
        hi = next_ref[k] + decode(down_ref[k, main:], from_above)[group : 2 * group]
        for f in far:
            beyond = (row > 1).astype(jnp.float32)
            lo += decode(f[k, main:], beyond)[2 * group : 3 * group]
        both = jnp.concatenate([lo, hi], axis=0)
        if edge_rows > 2 * group:
            both = jnp.concatenate([both] * (edge_rows // (2 * group)), axis=0)
        outs[k][main:] = encode(both)


def z_sum(p):
    lanes = index(p.shape, p.ndim - 1)
    before = jnp.where(lanes == 0, 0.0, pltpu.roll(p, 1, p.ndim - 1))
    after = jnp.where(lanes == 127, 0.0, pltpu.roll(p, 127, p.ndim - 1))
    return before + p + after


def two_classes(d1, d2):
    top = jnp.maximum(jnp.maximum(d1, d2), 0.0)
    e0, e1, e2 = jnp.exp2(-top), jnp.exp2(d1 - top), jnp.exp2(d2 - top)
    inverse = 1.0 / (e0 + e1 + e2)
    return e0 * inverse, e1 * inverse


def ends_of(dims, scal, here, there, pad):
    half, stride = dims["half"], dims["stride"]
    main = slice(2 * half * stride, None)
    d = decode(here[main], LOG2E) + decode(there[main], LOG2E)
    row = scal[1]
    for k, p in enumerate(two_classes(d, jnp.concatenate([d[half:], d[:half]], axis=0))):
        for u in range(half):
            lo, hi = p[u : u + 1], p[2 * half + u : 2 * half + u + 1]
            pad[u, k, 7:8] = jnp.where(row > 0, lo, 0.0)
            pad[u, k, 8 + stride : 9 + stride] = jnp.where(row < dims["rows_y"] - 1, hi, 0.0)


def halves_of(dims, here, there, u, pad):
    half, stride = dims["half"], dims["stride"]

    def total(j):
        part = pl.ds(pl.multiple_of(j * stride, stride), stride)
        return decode(here[part], LOG2E) + decode(there[part], LOG2E)

    sums = []
    for k, p in enumerate(two_classes(total(u), total(half + u))):
        at = pad.at[u, k]
        at[8 : 8 + stride] = p
        sums.append(z_sum(at[7 : 7 + stride] + p + at[9 : 9 + stride]))
    left = index((stride, 128), 1) < 64
    return (
        jnp.where(left, sums[0], pltpu.roll(sums[1], 64, 1)),
        jnp.where(left, pltpu.roll(sums[0], 64, 1), sums[1]),
    )


def edge_kernel(dims, scal, *refs):
    half, slabs = dims["half"], dims["slabs"]
    codes, ends, pad = refs[: 2 * slabs], refs[-2], refs[-1]
    g, core = scal[0], scal[2]
    low = core == 0
    at = (g & (slabs - 1)) ^ jnp.where(low, 0, slabs - 1)
    u = jnp.where(low, 0, half - 1)
    for s in range(slabs):

        @pl.when(at == s)
        def _():
            ends_of(dims, scal, codes[s], codes[s + slabs], pad)
            z0, z1 = halves_of(dims, codes[s], codes[s + slabs], u, pad)
            ends[0] = z0
            ends[1] = z1


def smooth_kernel(dims, scal, *refs):
    half, slabs = dims["half"], dims["slabs"]
    codes, keep, send, pad = refs[: 2 * slabs], refs[-3], refs[-2], refs[-1]
    g, core = scal[0], scal[2]
    low = core == 0
    for s in range(slabs):
        t = (g & (slabs - 1)) ^ s
        mine = pad.at[s]
        ends_of(dims, scal, codes[s], codes[s + slabs], mine)
        for u in range(half):
            z0, z1 = halves_of(dims, codes[s], codes[s + slabs], u, mine)
            keep[t, u] = jnp.where(low, z0, z1)
            send[t, u] = jnp.where(low, z1, z0)


def finish_kernel(dims, scal, keep, recv, mine, theirs, smooth, confidence):
    half, stride, slabs, depth = dims["half"], dims["stride"], dims["slabs"], dims["depth"]
    step = dims["step"]
    g, row, core = scal[0], scal[1], scal[2]
    low = core == 0
    t = pl.program_id(0) * step

    def lower(at, u):
        return jnp.where(low, keep[at, u], recv[at, u])

    def higher(at, u):
        return jnp.where(low, recv[at, u], keep[at, u])

    first = jnp.where(low, theirs[core], mine[core])
    last = jnp.where(low, mine[core], theirs[core])
    lines = [jnp.where(t > 0, higher(jnp.maximum(t - 1, 0), half - 1), first)]
    for i in range(step):
        lines += [lower(t + i, u) for u in range(half)]
        lines += [higher(t + i, u) for u in range(half)]
    end = t + step
    lines += [jnp.where(end < slabs, lower(jnp.minimum(end, slabs - 1), 0), last)]
    shape = (stride, 128)
    y = row * stride + index(shape, 0)
    z = core * depth + (index(shape, 1) & (depth - 1))

    def line_count(cell, extent):
        return 3.0 - (cell == 0).astype(jnp.float32) - (cell == extent - 1).astype(jnp.float32)

    inverse = 1.0 / (line_count(y, dims["rows_y"] * stride) * line_count(z, 2 * depth))
    for i in range(2 * half * step):
        x = jnp.full((8, 128), g * stride + t * 2 * half + i)
        scale = 1.0 / line_count(x, dims["extent_x"])
        total = (lines[i] + lines[i + 1] + lines[i + 2]) * inverse
        total = (total.reshape(-1, 8, 128) * scale).reshape(shape)
        c0 = total[:, :depth]
        c1 = pltpu.roll(total, 64, 1)[:, :depth]
        c2 = jnp.maximum(1.0 - (c0 + c1), 0.0)
        smooth[0, i] = c0
        smooth[1, i] = c1
        smooth[2, i] = c2
        confidence[i] = jnp.maximum(jnp.maximum(c0, c1), c2)


def vmem(*shape):
    return pltpu.VMEM(shape, jnp.float32)


def whole(shape):
    return pl.BlockSpec(shape, lambda *_: (0,) * len(shape))


def like(shape, dtype=jnp.float32):
    return jax.ShapeDtypeStruct(shape, dtype)


def call(kernel, scal, args, outs, in_specs=None, out_specs=None, grid=(1,), scratch=(),
         mib=4, flops=0):
    args = list(args)
    size = sum(a.size * a.dtype.itemsize for a in args + list(outs))
    return pl.pallas_call(
        kernel,
        out_shape=list(outs),
        grid_spec=pltpu.PrefetchScalarGridSpec(
            num_scalar_prefetch=1,
            grid=grid,
            in_specs=in_specs or [whole(a.shape) for a in args],
            out_specs=out_specs or [whole(o.shape) for o in outs],
            scratch_shapes=list(scratch),
        ),
        compiler_params=pltpu.CompilerParams(vmem_limit_bytes=int(mib * 2**20)),
        cost_estimate=pl.CostEstimate(flops=flops, bytes_accessed=size, transcendentals=0),
    )(scal, *args)


def stitched(patches):
    positions, per_y, classes, slab, length, lanes = patches.shape
    nx_dev, ny_dev, nz_dev = (lax.axis_size(n) for n in ("gx", "gy", "gz"))
    stride = length // 2
    half = slab // nz_dev
    assert positions == nx_dev and per_y == 1 and classes == 3 and nz_dev == 2
    assert lanes == 128 and length == 64
    slabs = nx_dev // 2
    depth = lanes // 2
    far = int(ny_dev > 2)
    edge, edge_y = (-(-n * 2 * half // 16) * 16 for n in (2, 2 + far))
    main = 2 * half * stride
    rows, rows_up = main + edge, main + edge_y
    g, row, core = (lax.axis_index(n) for n in ("gx", "gy", "gz"))
    scal = jnp.stack([g, row, core]).astype(jnp.int32)
    dims = dict(
        length=length, half=half, stride=stride, slabs=slabs, rows=rows, edge=edge, far=far,
        rows_y=ny_dev, depth=depth, extent_x=positions * stride,
        lines=(stride - 1, 0) + (length - 1,) * far,
    )
    weights = jnp.asarray(z_weights(length, depth))

    def ship(array, axis, by):
        size = lax.axis_size(axis)
        pairs = [(i, i + by) for i in range(size) if 0 <= i + by < size]
        return lax.ppermute(array, axis, pairs)

    def upper(g, core):
        return ((g * 2 + core) * half >= stride).astype(jnp.int32)

    def swapped(first):
        def base(g, core):
            start = ((g ^ first) & ~(slabs - 1)) - upper(g, core)
            return jnp.clip(start, 0, positions - slabs)

        (other,) = call(
            functools.partial(pick_kernel, dict(dims, count=slabs, base=base)), scal,
            [patches], [like((slabs, 1, 3, half, length, 128), jnp.bfloat16)],
            in_specs=[pl.BlockSpec(memory_space=pl.ANY)],
            scratch=[pltpu.SemaphoreType.DMA(())],
        )
        return lax.ppermute(other, "gz", [(0, 1), (1, 0)]), base

    def messages(first, count, recv, base):
        d = dict(dims, first=first, count=count, base=base)
        own, up, ahead = call(
            functools.partial(fold_kernel, d), scal, [patches, recv, weights],
            [
                like((count, 2 * half, stride, 128)),
                like((count, rows_up, 128), jnp.bfloat16),
                like((count, 2 * half, 128)),
            ],
            scratch=[vmem(length, 128), vmem(edge_y, 128)],
        )
        if ny_dev == 2:
            below = above = lax.ppermute(up, "gy", [(0, 1), (1, 0)])
        else:
            below, above = ship(up, "gy", 1), ship(up, "gy", -1)
        beyond = [ship(up, "gy", 2)] * far
        parts = call(
            functools.partial(join_kernel, d), scal,
            [own, ahead, below, above] + beyond,
            [like((rows, 128), jnp.bfloat16)] * count,
        )
        return [
            lax.ppermute(p, "gx", [(i, i ^ s) for i in range(nx_dev)]) if s else p
            for s, p in enumerate(parts, first)
        ]

    recv_far = swapped(slabs)
    recv_near = swapped(0)
    first = messages(slabs, slabs // 2, *recv_far)
    second = messages(slabs + slabs // 2, slabs // 2, *recv_far)
    third = messages(0, slabs, *recv_near)
    codes = third + first + second

    half_rows = (slabs, half, stride, 128)
    (ends,) = call(
        functools.partial(edge_kernel, dims), scal, codes, [like((2, stride, 128))],
        scratch=[vmem(half, 2, stride + 16, 128)],
    )
    above = [(2 * i + 1, 2 * i + 3) for i in range(nx_dev - 1)]
    below = [(2 * i + 2, 2 * i) for i in range(nx_dev - 1)]
    mine = lax.ppermute(ends, ("gx", "gz"), above + below)
    codes, _ = lax.optimization_barrier((codes, ends))
    keep, send = call(
        functools.partial(smooth_kernel, dims), scal, codes, [like(half_rows)] * 2,
        scratch=[vmem(slabs, half, 2, stride + 16, 128)],
    )
    recv = lax.ppermute(send, "gz", [(0, 1), (1, 0)])
    theirs = lax.ppermute(mine, "gz", [(0, 1), (1, 0)])

    step = slabs // 2
    return tuple(
        call(
            functools.partial(finish_kernel, dict(dims, step=step)), scal,
            [keep, recv, mine, theirs],
            [like((3, stride, stride, depth)), like((stride, stride, depth))],
            out_specs=[
                pl.BlockSpec((3, 2 * half * step, stride, depth), lambda i, s: (0, i, 0, 0)),
                pl.BlockSpec((2 * half * step, stride, depth), lambda i, s: (i, 0, 0)),
            ],
            grid=(slabs // step,),
            mib=8,
        )
    )


def solution(mesh):
    in_specs = (P(None, "gy", None, "gx", None, "gz"),)
    out_specs = (P(None, "gx", "gy", "gz"), P("gx", "gy", "gz"))
    return jax.shard_map(
        stitched, mesh=mesh, in_specs=in_specs, out_specs=out_specs, check_vma=False
    )
```

```python
import functools
import math

import jax
import jax.numpy as jnp
import numpy as np
from jax import lax
from jax.experimental import pallas as pl
from jax.experimental.pallas import tpu as pltpu
from jax.sharding import PartitionSpec as P


KNEE = 0.5
BASE = 2.0**-5
POWER = 17
LOG2E = 1.4426950408889634


def encode(d):
    t = d * (BASE / KNEE) + jnp.where(d < 0.0, -BASE, BASE)
    p = t
    for _ in range(4):
        p = p * p
    return (p * t).astype(jnp.bfloat16)


def decode(code, scale=1.0):
    v = code.astype(jnp.float32)
    t = jnp.exp2(jnp.log(jnp.abs(v)) * (LOG2E / POWER))
    k = scale * (KNEE / BASE)
    return (t - BASE) * jnp.where(v < 0.0, -k, k)


def share(cell, length, paired):
    stride = length // 2
    centre, spread = (length - 1) / 2.0, length / 8.0
    other = jnp.where(cell < stride, cell + stride, cell - stride).astype(jnp.float32)
    mine = cell.astype(jnp.float32)
    ratio = ((mine - centre) ** 2 - (other - centre) ** 2) / (2.0 * spread * spread)
    alone = jnp.logical_and(cell < stride, jnp.logical_not(paired))
    return jnp.where(alone, 1.0, 1.0 / (1.0 + jnp.exp(ratio)))


def z_weights(length, depth):
    stride, count = length // 2, 2 * depth // (length // 2)
    u = np.arange(length, dtype=np.float64)
    g = np.exp(-((u - (length - 1) / 2.0) ** 2) / (2.0 * (length / 8.0) ** 2))
    table = np.zeros((count * length, 2 * depth), np.float32)
    for k in range(count):
        for w in range(length):
            z = k * stride + w
            if z < 2 * depth:
                alone = k == 0 and w < stride
                pair = 0.0 if alone else g[w + stride if w < stride else w - stride]
                table[k * length + w, z] = g[w] / (g[w] + pair)
    high = table.astype(jnp.bfloat16)
    low = (table - high.astype(np.float32)).astype(jnp.bfloat16)
    both = np.concatenate([high, low], 1)
    return np.stack([both, np.roll(both, count * length // 2, 0)])


def index(shape, axis):
    return lax.broadcasted_iota(jnp.int32, shape, axis)


def pick_kernel(dims, scal, patches, out, sem):
    count, half = dims["count"], dims["half"]
    start = dims["base"](scal[0], scal[2])
    rows = pl.ds((1 - scal[2]) * half, half)
    copy = pltpu.make_async_copy(patches.at[pl.ds(start, count), :, :, rows], out, sem)
    copy.start()
    copy.wait()


def fold_kernel(dims, scal, own_ref, recv_ref, w_ref, own_out, up_out, next_out, ny, edge):
    length, half, stride, first = dims["length"], dims["half"], dims["stride"], dims["first"]
    g, row, core = scal[0], scal[1], scal[2]
    begin = (g * 2 + core) * half
    upper = (begin >= stride).astype(jnp.int32)
    cell = index((length, 128), 0)
    ny[...] = share(cell, length, jnp.full(cell.shape, row) > 0)
    edge[...] = jnp.zeros_like(edge)
    shape = (8, 128)
    nx_pair = [
        share(jnp.full(shape, begin + u), length, jnp.full(shape, 1) > 0) for u in range(half)
    ]
    weights = w_ref[core]

    def body(i, carry):
        a = (g ^ (first + i)) - upper
        at = jnp.maximum(a, 0)
        recv_at = at - dims["base"](g, core)
        for u in range(half):
            nx = jnp.where(jnp.logical_and(a == 0, upper == 0), 1.0, nx_pair[u])
            nx = jnp.where(a < 0, 0.0, nx)
            both = (ny[...].reshape(-1, 8, 128) * nx).reshape(length, 128)
            rows = [
                jnp.concatenate([own_ref[at, 0, k, core * half + u], recv_ref[recv_at, 0, k, u]], 1)
                for k in range(3)
            ]
            part = jnp.dot(
                jnp.concatenate(rows, 0), weights, preferred_element_type=jnp.float32
            )
            part = part[:, :128] + part[:, 128:]
            for k in range(2):
                total = (part[(k + 1) * length : (k + 2) * length] - part[:length]) * both
                j = k * half + u
                own_out[i, j] = total[:stride]
                up_out[i, j * stride : (j + 1) * stride] = encode(total[stride:])
                for n, line in enumerate(dims["lines"]):
                    edge[2 * half * n + j : 2 * half * n + j + 1] = total[line : line + 1]
                next_out[i, j : j + 1] = total[stride : stride + 1]
        up_out[i, 2 * half * stride :] = encode(edge[...])
        return carry

    lax.fori_loop(0, dims["count"], body, 0, unroll=2)


def join_kernel(dims, scal, own_ref, next_ref, up_ref, down_ref, *refs):
    half, stride, count, edge_rows = dims["half"], dims["stride"], dims["count"], dims["edge"]
    far = refs[:-count]
    outs = refs[len(far) : len(far) + count]
    row, rows_y = scal[1], dims["rows_y"]
    from_below = (row > 0).astype(jnp.float32)
    from_above = (row < rows_y - 1).astype(jnp.float32)
    main, group = 2 * half * stride, 2 * half

    def body(j, carry):
        part = pl.ds(pl.multiple_of(j * stride, stride), stride)
        for k in range(count):
            outs[k][part] = encode(own_ref[k, j] + decode(up_ref[k, part], from_below))
        return carry

    lax.fori_loop(0, 2 * half, body, 0)
    for k in range(count):
        lo = decode(up_ref[k, main:], from_below)[:group]
        hi = next_ref[k] + decode(down_ref[k, main:], from_above)[group : 2 * group]
        for f in far:
            beyond = (row > 1).astype(jnp.float32)
            lo += decode(f[k, main:], beyond)[2 * group : 3 * group]
        both = jnp.concatenate([lo, hi], axis=0)
        if edge_rows > 2 * group:
            both = jnp.concatenate([both] * (edge_rows // (2 * group)), axis=0)
        outs[k][main:] = encode(both)


def z_sum(p):
    lanes = index(p.shape, p.ndim - 1)
    before = jnp.where(lanes == 0, 0.0, pltpu.roll(p, 1, p.ndim - 1))
    after = jnp.where(lanes == 127, 0.0, pltpu.roll(p, 127, p.ndim - 1))
    return before + p + after


def two_classes(d1, d2):
    top = jnp.maximum(jnp.maximum(d1, d2), 0.0)
    e0, e1, e2 = jnp.exp2(-top), jnp.exp2(d1 - top), jnp.exp2(d2 - top)
    inverse = 1.0 / (e0 + e1 + e2)
    return e0 * inverse, e1 * inverse


def ends_of(dims, scal, here, there, pad):
    half, stride = dims["half"], dims["stride"]
    main = slice(2 * half * stride, None)
    d = decode(here[main], LOG2E) + decode(there[main], LOG2E)
    row = scal[1]
    for k, p in enumerate(two_classes(d, jnp.concatenate([d[half:], d[:half]], axis=0))):
        for u in range(half):
            lo, hi = p[u : u + 1], p[2 * half + u : 2 * half + u + 1]
            pad[u, k, 7:8] = jnp.where(row > 0, lo, 0.0)
            pad[u, k, 8 + stride : 9 + stride] = jnp.where(row < dims["rows_y"] - 1, hi, 0.0)


def halves_of(dims, here, there, u, pad):
    half, stride = dims["half"], dims["stride"]

    def total(j):
        part = pl.ds(pl.multiple_of(j * stride, stride), stride)
        return decode(here[part], LOG2E) + decode(there[part], LOG2E)

    sums = []
    for k, p in enumerate(two_classes(total(u), total(half + u))):
        at = pad.at[u, k]
        at[8 : 8 + stride] = p
        sums.append(z_sum(at[7 : 7 + stride] + p + at[9 : 9 + stride]))
    left = index((stride, 128), 1) < 64
    return (
        jnp.where(left, sums[0], pltpu.roll(sums[1], 64, 1)),
        jnp.where(left, pltpu.roll(sums[0], 64, 1), sums[1]),
    )


def edge_kernel(dims, scal, *refs):
    half, slabs = dims["half"], dims["slabs"]
    codes, ends, pad = refs[: 2 * slabs], refs[-2], refs[-1]
    g, core = scal[0], scal[2]
    low = core == 0
    at = (g & (slabs - 1)) ^ jnp.where(low, 0, slabs - 1)
    u = jnp.where(low, 0, half - 1)
    for s in range(slabs):

        @pl.when(at == s)
        def _():
            ends_of(dims, scal, codes[s], codes[s + slabs], pad)
            z0, z1 = halves_of(dims, codes[s], codes[s + slabs], u, pad)
            ends[0] = z0
            ends[1] = z1


def smooth_kernel(dims, scal, *refs):
    half, slabs = dims["half"], dims["slabs"]
    codes, keep, send, pad = refs[: 2 * slabs], refs[-3], refs[-2], refs[-1]
    g, core = scal[0], scal[2]
    low = core == 0
    for s in range(slabs):
        t = (g & (slabs - 1)) ^ s
        mine = pad.at[s]
        ends_of(dims, scal, codes[s], codes[s + slabs], mine)
        for u in range(half):
            z0, z1 = halves_of(dims, codes[s], codes[s + slabs], u, mine)
            keep[t, u] = jnp.where(low, z0, z1)
            send[t, u] = jnp.where(low, z1, z0)


def finish_kernel(dims, scal, keep, recv, mine, theirs, smooth, confidence):
    half, stride, slabs, depth = dims["half"], dims["stride"], dims["slabs"], dims["depth"]
    step = dims["step"]
    g, row, core = scal[0], scal[1], scal[2]
    low = core == 0
    t = pl.program_id(0) * step

    def lower(at, u):
        return jnp.where(low, keep[at, u], recv[at, u])

    def higher(at, u):
        return jnp.where(low, recv[at, u], keep[at, u])

    first = jnp.where(low, theirs[core], mine[core])
    last = jnp.where(low, mine[core], theirs[core])
    lines = [jnp.where(t > 0, higher(jnp.maximum(t - 1, 0), half - 1), first)]
    for i in range(step):
        lines += [lower(t + i, u) for u in range(half)]
        lines += [higher(t + i, u) for u in range(half)]
    end = t + step
    lines += [jnp.where(end < slabs, lower(jnp.minimum(end, slabs - 1), 0), last)]
    shape = (stride, 128)
    y = row * stride + index(shape, 0)
    z = core * depth + (index(shape, 1) & (depth - 1))

    def line_count(cell, extent):
        return 3.0 - (cell == 0).astype(jnp.float32) - (cell == extent - 1).astype(jnp.float32)

    inverse = 1.0 / (line_count(y, dims["rows_y"] * stride) * line_count(z, 2 * depth))
    for i in range(2 * half * step):
        x = jnp.full((8, 128), g * stride + t * 2 * half + i)
        scale = 1.0 / line_count(x, dims["extent_x"])
        total = (lines[i] + lines[i + 1] + lines[i + 2]) * inverse
        total = (total.reshape(-1, 8, 128) * scale).reshape(shape)
        c0 = total[:, :depth]
        c1 = pltpu.roll(total, 64, 1)[:, :depth]
        c2 = jnp.maximum(1.0 - (c0 + c1), 0.0)
        smooth[0, i] = c0
        smooth[1, i] = c1
        smooth[2, i] = c2
        confidence[i] = jnp.maximum(jnp.maximum(c0, c1), c2)


def vmem(*shape):
    return pltpu.VMEM(shape, jnp.float32)


def whole(shape):
    return pl.BlockSpec(shape, lambda *_: (0,) * len(shape))


def like(shape, dtype=jnp.float32):
    return jax.ShapeDtypeStruct(shape, dtype)


def call(kernel, scal, args, outs, in_specs=None, out_specs=None, grid=(1,), scratch=(),
         mib=4, flops=0):
    args = list(args)
    size = sum(math.prod(a.shape) * a.dtype.itemsize for a in args + list(outs))
    return pl.pallas_call(
        kernel,
        out_shape=list(outs),
        grid_spec=pltpu.PrefetchScalarGridSpec(
            num_scalar_prefetch=1,
            grid=grid,
            in_specs=in_specs or [whole(a.shape) for a in args],
            out_specs=out_specs or [whole(o.shape) for o in outs],
            scratch_shapes=list(scratch),
        ),
        compiler_params=pltpu.CompilerParams(vmem_limit_bytes=int(mib * 2**20)),
        cost_estimate=pl.CostEstimate(flops=flops, bytes_accessed=size, transcendentals=0),
    )(scal, *args)


def stitched(patches):
    positions, per_y, classes, slab, length, lanes = patches.shape
    nx_dev, ny_dev, nz_dev = (lax.axis_size(n) for n in ("gx", "gy", "gz"))
    stride = length // 2
    half = slab // nz_dev
    assert positions == nx_dev and per_y == 1 and classes == 3 and nz_dev == 2
    assert lanes == 128 and length == 64
    slabs = nx_dev // 2
    depth = lanes // 2
    far = int(ny_dev > 2)
    edge, edge_y = (-(-n * 2 * half // 16) * 16 for n in (2, 2 + far))
    main = 2 * half * stride
    rows, rows_up = main + edge, main + edge_y
    g, row, core = (lax.axis_index(n) for n in ("gx", "gy", "gz"))
    scal = jnp.stack([g, row, core]).astype(jnp.int32)
    dims = dict(
        length=length, half=half, stride=stride, slabs=slabs, rows=rows, edge=edge, far=far,
        rows_y=ny_dev, depth=depth, extent_x=positions * stride,
        lines=(stride - 1, 0) + (length - 1,) * far,
    )
    weights = jnp.asarray(z_weights(length, depth))

    def ship(array, axis, by):
        size = lax.axis_size(axis)
        pairs = [(i, i + by) for i in range(size) if 0 <= i + by < size]
        return lax.ppermute(array, axis, pairs)

    def upper(g, core):
        return ((g * 2 + core) * half >= stride).astype(jnp.int32)

    def swapped(first):
        def base(g, core):
            start = ((g ^ first) & ~(slabs - 1)) - upper(g, core)
            return jnp.clip(start, 0, positions - slabs)

        shape = (slabs, 1, 3, half, length, 128)
        (other,) = call(
            functools.partial(pick_kernel, dict(dims, count=slabs, base=base)), scal,
            [pltpu.with_memory_space_constraint(patches, pltpu.HBM) if first else patches],
            [pltpu.VMEM(shape, jnp.bfloat16)],
            in_specs=[pl.BlockSpec(memory_space=pl.ANY)],
            out_specs=[pl.BlockSpec(memory_space=pltpu.VMEM)],
            scratch=[pltpu.SemaphoreType.DMA(())],
        )
        return lax.ppermute(other, "gz", [(0, 1), (1, 0)]), base

    def messages(first, count, recv, base):
        d = dict(dims, first=first, count=count, base=base)
        own, up, ahead = call(
            functools.partial(fold_kernel, d), scal, [patches, recv, weights],
            [
                like((count, 2 * half, stride, 128)),
                like((count, rows_up, 128), jnp.bfloat16),
                like((count, 2 * half, 128)),
            ],
            scratch=[vmem(length, 128), vmem(edge_y, 128)],
        )
        if ny_dev == 2:
            below = above = lax.ppermute(up, "gy", [(0, 1), (1, 0)])
        else:
            below, above = ship(up, "gy", 1), ship(up, "gy", -1)
        beyond = [ship(up, "gy", 2)] * far
        parts = call(
            functools.partial(join_kernel, d), scal,
            [own, ahead, below, above] + beyond,
            [like((rows, 128), jnp.bfloat16)] * count,
        )
        return [
            lax.ppermute(p, "gx", [(i, i ^ s) for i in range(nx_dev)]) if s else p
            for s, p in enumerate(parts, first)
        ]

    recv_far = swapped(slabs)
    recv_near = swapped(0)
    first = messages(slabs, slabs // 2, *recv_far)
    second = messages(slabs + slabs // 2, slabs // 2, *recv_far)
    third = messages(0, slabs, *recv_near)
    codes = third + first + second

    half_rows = (slabs, half, stride, 128)
    (ends,) = call(
        functools.partial(edge_kernel, dims), scal, codes, [like((2, stride, 128))],
        scratch=[vmem(half, 2, stride + 16, 128)],
    )
    above = [(2 * i + 1, 2 * i + 3) for i in range(nx_dev - 1)]
    below = [(2 * i + 2, 2 * i) for i in range(nx_dev - 1)]
    mine = lax.ppermute(ends, ("gx", "gz"), above + below)
    codes, _ = lax.optimization_barrier((codes, ends))
    keep, send = call(
        functools.partial(smooth_kernel, dims), scal, codes, [like(half_rows)] * 2,
        scratch=[vmem(slabs, half, 2, stride + 16, 128)],
    )
    recv = lax.ppermute(send, "gz", [(0, 1), (1, 0)])
    theirs = lax.ppermute(mine, "gz", [(0, 1), (1, 0)])

    step = slabs // 2
    return tuple(
        call(
            functools.partial(finish_kernel, dict(dims, step=step)), scal,
            [keep, recv, mine, theirs],
            [like((3, stride, stride, depth)), like((stride, stride, depth))],
            out_specs=[
                pl.BlockSpec((3, 2 * half * step, stride, depth), lambda i, s: (0, i, 0, 0)),
                pl.BlockSpec((2 * half * step, stride, depth), lambda i, s: (i, 0, 0)),
            ],
            grid=(slabs // step,),
            mib=8,
        )
    )


def solution(mesh):
    in_specs = (P(None, "gy", None, "gx", None, "gz"),)
    out_specs = (P(None, "gx", "gy", "gz"), P("gx", "gy", "gz"))
    return jax.shard_map(
        stitched, mesh=mesh, in_specs=in_specs, out_specs=out_specs, check_vma=False
    )
```

```python
import functools
import math

import jax
import jax.numpy as jnp
import numpy as np
from jax import lax
from jax.experimental import pallas as pl
from jax.experimental.pallas import tpu as pltpu
from jax.sharding import PartitionSpec as P


KNEE = 2.0
BASE = 2.0 ** (-120 / 33)
POWER = 33
LOG2E = 1.4426950408889634


def encode(d):
    t = d * (BASE / KNEE) + jnp.where(d < 0.0, -BASE, BASE)
    p = t
    for _ in range(5):
        p = p * p
    return (p * t).astype(jnp.bfloat16)


def decode(code, scale=1.0):
    v = code.astype(jnp.float32)
    t = jnp.exp2(jnp.log(jnp.abs(v)) * (LOG2E / POWER))
    k = scale * (KNEE / BASE)
    return (t - BASE) * jnp.where(v < 0.0, -k, k)


def share(cell, length, paired):
    stride = length // 2
    centre, spread = (length - 1) / 2.0, length / 8.0
    other = jnp.where(cell < stride, cell + stride, cell - stride).astype(jnp.float32)
    mine = cell.astype(jnp.float32)
    ratio = ((mine - centre) ** 2 - (other - centre) ** 2) / (2.0 * spread * spread)
    alone = jnp.logical_and(cell < stride, jnp.logical_not(paired))
    return jnp.where(alone, 1.0, 1.0 / (1.0 + jnp.exp(ratio)))


def z_weights(length, depth):
    stride, count = length // 2, 2 * depth // (length // 2)
    u = np.arange(length, dtype=np.float64)
    g = np.exp(-((u - (length - 1) / 2.0) ** 2) / (2.0 * (length / 8.0) ** 2))
    table = np.zeros((count * length, 2 * depth), np.float32)
    for k in range(count):
        for w in range(length):
            z = k * stride + w
            if z < 2 * depth:
                alone = k == 0 and w < stride
                pair = 0.0 if alone else g[w + stride if w < stride else w - stride]
                table[k * length + w, z] = g[w] / (g[w] + pair)
    high = table.astype(jnp.bfloat16)
    low = (table - high.astype(np.float32)).astype(jnp.bfloat16)
    both = np.concatenate([high, low], 1)
    return np.stack([both, np.roll(both, count * length // 2, 0)])


def index(shape, axis):
    return lax.broadcasted_iota(jnp.int32, shape, axis)


def pick_kernel(dims, scal, patches, out, sem):
    count, half = dims["count"], dims["half"]
    start = dims["base"](scal[0], scal[2])
    rows = pl.ds((1 - scal[2]) * half, half)
    copy = pltpu.make_async_copy(patches.at[pl.ds(start, count), :, :, rows], out, sem)
    copy.start()
    copy.wait()


def fold_kernel(dims, scal, own_ref, recv_ref, w_ref, own_out, up_out, next_out, ny, edge):
    length, half, stride, first = dims["length"], dims["half"], dims["stride"], dims["first"]
    g, row, core = scal[0], scal[1], scal[2]
    begin = (g * 2 + core) * half
    upper = (begin >= stride).astype(jnp.int32)
    cell = index((length, 128), 0)
    ny[...] = share(cell, length, jnp.full(cell.shape, row) > 0)
    edge[...] = jnp.zeros_like(edge)
    shape = (8, 128)
    nx_pair = [
        share(jnp.full(shape, begin + u), length, jnp.full(shape, 1) > 0) for u in range(half)
    ]
    weights = w_ref[core]

    def body(i, carry):
        a = (g ^ (first + i)) - upper
        at = jnp.maximum(a, 0)
        recv_at = at - dims["base"](g, core)
        for u in range(half):
            nx = jnp.where(jnp.logical_and(a == 0, upper == 0), 1.0, nx_pair[u])
            nx = jnp.where(a < 0, 0.0, nx)
            both = (ny[...].reshape(-1, 8, 128) * nx).reshape(length, 128)
            rows = [
                jnp.concatenate([own_ref[at, 0, k, core * half + u], recv_ref[recv_at, 0, k, u]], 1)
                for k in range(3)
            ]
            part = jnp.dot(
                jnp.concatenate(rows, 0), weights, preferred_element_type=jnp.float32
            )
            part = part[:, :128] + part[:, 128:]
            for k in range(2):
                total = (part[(k + 1) * length : (k + 2) * length] - part[:length]) * both
                j = k * half + u
                own_out[i, j] = total[:stride]
                up_out[i, j * stride : (j + 1) * stride] = encode(total[stride:])
                for n, line in enumerate(dims["lines"]):
                    edge[2 * half * n + j : 2 * half * n + j + 1] = total[line : line + 1]
                next_out[i, j : j + 1] = total[stride : stride + 1]
        up_out[i, 2 * half * stride :] = encode(edge[...])
        return carry

    lax.fori_loop(0, dims["count"], body, 0, unroll=2)


def join_kernel(dims, scal, own_ref, next_ref, up_ref, down_ref, *refs):
    half, stride, count, edge_rows = dims["half"], dims["stride"], dims["count"], dims["edge"]
    far = refs[:-count]
    outs = refs[len(far) : len(far) + count]
    row, rows_y = scal[1], dims["rows_y"]
    from_below = (row > 0).astype(jnp.float32)
    from_above = (row < rows_y - 1).astype(jnp.float32)
    main, group = 2 * half * stride, 2 * half

    def body(j, carry):
        part = pl.ds(pl.multiple_of(j * stride, stride), stride)
        for k in range(count):
            outs[k][part] = encode(own_ref[k, j] + decode(up_ref[k, part], from_below))
        return carry

    lax.fori_loop(0, 2 * half, body, 0, unroll=4)
    for k in range(count):
        lo = decode(up_ref[k, main:], from_below)[:group]
        hi = next_ref[k] + decode(down_ref[k, main:], from_above)[group : 2 * group]
        for f in far:
            beyond = (row > 1).astype(jnp.float32)
            lo += decode(f[k, main:], beyond)[2 * group : 3 * group]
        both = jnp.concatenate([lo, hi], axis=0)
        if edge_rows > 2 * group:
            both = jnp.concatenate([both] * (edge_rows // (2 * group)), axis=0)
        outs[k][main:] = encode(both)


def z_sum(p):
    lanes = index(p.shape, p.ndim - 1)
    before = jnp.where(lanes == 0, 0.0, pltpu.roll(p, 1, p.ndim - 1))
    after = jnp.where(lanes == 127, 0.0, pltpu.roll(p, 127, p.ndim - 1))
    return before + p + after


def two_classes(d1, d2):
    top = jnp.maximum(jnp.maximum(d1, d2), 0.0)
    e0, e1, e2 = jnp.exp2(-top), jnp.exp2(d1 - top), jnp.exp2(d2 - top)
    inverse = 1.0 / (e0 + e1 + e2)
    return e0 * inverse, e1 * inverse


def ends_of(dims, scal, here, there, pad):
    half, stride = dims["half"], dims["stride"]
    main = slice(2 * half * stride, None)
    d = decode(here[main], LOG2E) + decode(there[main], LOG2E)
    row = scal[1]
    for k, p in enumerate(two_classes(d, jnp.concatenate([d[half:], d[:half]], axis=0))):
        for u in range(half):
            lo, hi = p[u : u + 1], p[2 * half + u : 2 * half + u + 1]
            pad[u, k, 7:8] = jnp.where(row > 0, lo, 0.0)
            pad[u, k, 8 + stride : 9 + stride] = jnp.where(row < dims["rows_y"] - 1, hi, 0.0)


def halves_of(dims, here, there, u, pad):
    half, stride = dims["half"], dims["stride"]

    def total(j):
        part = pl.ds(pl.multiple_of(j * stride, stride), stride)
        return decode(here[part], LOG2E) + decode(there[part], LOG2E)

    sums = []
    for k, p in enumerate(two_classes(total(u), total(half + u))):
        at = pad.at[u, k]
        at[8 : 8 + stride] = p
        sums.append(z_sum(at[7 : 7 + stride] + p + at[9 : 9 + stride]))
    left = index((stride, 128), 1) < 64
    return (
        jnp.where(left, sums[0], pltpu.roll(sums[1], 64, 1)),
        jnp.where(left, pltpu.roll(sums[0], 64, 1), sums[1]),
    )


def edge_kernel(dims, scal, *refs):
    half, slabs = dims["half"], dims["slabs"]
    codes, ends, pad = refs[: 2 * slabs], refs[-2], refs[-1]
    g, core = scal[0], scal[2]
    low = core == 0
    at = (g & (slabs - 1)) ^ jnp.where(low, 0, slabs - 1)
    u = jnp.where(low, 0, half - 1)
    for s in range(slabs):

        @pl.when(at == s)
        def _():
            ends_of(dims, scal, codes[s], codes[s + slabs], pad)
            z0, z1 = halves_of(dims, codes[s], codes[s + slabs], u, pad)
            ends[0] = z0
            ends[1] = z1


def smooth_kernel(dims, scal, *refs):
    half, slabs = dims["half"], dims["slabs"]
    codes, keep, send, pad = refs[: 2 * slabs], refs[-3], refs[-2], refs[-1]
    g, core = scal[0], scal[2]
    low = core == 0
    for s in range(slabs):
        t = (g & (slabs - 1)) ^ s
        mine = pad.at[s]
        ends_of(dims, scal, codes[s], codes[s + slabs], mine)
        for u in range(half):
            z0, z1 = halves_of(dims, codes[s], codes[s + slabs], u, mine)
            keep[t, u] = jnp.where(low, z0, z1)
            send[t, u] = jnp.where(low, z1, z0)


def finish_kernel(dims, scal, keep, recv, mine, theirs, smooth, confidence):
    half, stride, slabs, depth = dims["half"], dims["stride"], dims["slabs"], dims["depth"]
    step = dims["step"]
    g, row, core = scal[0], scal[1], scal[2]
    low = core == 0
    t = pl.program_id(0) * step

    def lower(at, u):
        return jnp.where(low, keep[at, u], recv[at, u])

    def higher(at, u):
        return jnp.where(low, recv[at, u], keep[at, u])

    first = jnp.where(low, theirs[core], mine[core])
    last = jnp.where(low, mine[core], theirs[core])
    lines = [jnp.where(t > 0, higher(jnp.maximum(t - 1, 0), half - 1), first)]
    for i in range(step):
        lines += [lower(t + i, u) for u in range(half)]
        lines += [higher(t + i, u) for u in range(half)]
    end = t + step
    lines += [jnp.where(end < slabs, lower(jnp.minimum(end, slabs - 1), 0), last)]
    shape = (stride, 128)
    y = row * stride + index(shape, 0)
    z = core * depth + (index(shape, 1) & (depth - 1))

    def line_count(cell, extent):
        return 3.0 - (cell == 0).astype(jnp.float32) - (cell == extent - 1).astype(jnp.float32)

    inverse = 1.0 / (line_count(y, dims["rows_y"] * stride) * line_count(z, 2 * depth))
    for i in range(2 * half * step):
        x = jnp.full((8, 128), g * stride + t * 2 * half + i)
        scale = 1.0 / line_count(x, dims["extent_x"])
        total = (lines[i] + lines[i + 1] + lines[i + 2]) * inverse
        total = (total.reshape(-1, 8, 128) * scale).reshape(shape)
        c0 = total[:, :depth]
        c1 = pltpu.roll(total, 64, 1)[:, :depth]
        c2 = jnp.maximum(1.0 - (c0 + c1), 0.0)
        smooth[0, i] = c0
        smooth[1, i] = c1
        smooth[2, i] = c2
        confidence[i] = jnp.maximum(jnp.maximum(c0, c1), c2)


def vmem(*shape):
    return pltpu.VMEM(shape, jnp.float32)


def whole(shape):
    return pl.BlockSpec(shape, lambda *_: (0,) * len(shape))


def like(shape, dtype=jnp.float32):
    return jax.ShapeDtypeStruct(shape, dtype)


def call(kernel, scal, args, outs, in_specs=None, out_specs=None, grid=(1,), scratch=(),
         mib=4, flops=0):
    args = list(args)
    size = sum(math.prod(a.shape) * a.dtype.itemsize for a in args + list(outs))
    return pl.pallas_call(
        kernel,
        out_shape=list(outs),
        grid_spec=pltpu.PrefetchScalarGridSpec(
            num_scalar_prefetch=1,
            grid=grid,
            in_specs=in_specs or [whole(a.shape) for a in args],
            out_specs=out_specs or [whole(o.shape) for o in outs],
            scratch_shapes=list(scratch),
        ),
        compiler_params=pltpu.CompilerParams(vmem_limit_bytes=int(mib * 2**20)),
        cost_estimate=pl.CostEstimate(flops=flops, bytes_accessed=size, transcendentals=0),
    )(scal, *args)


def stitched(patches):
    positions, per_y, classes, slab, length, lanes = patches.shape
    nx_dev, ny_dev, nz_dev = (lax.axis_size(n) for n in ("gx", "gy", "gz"))
    stride = length // 2
    half = slab // nz_dev
    assert positions == nx_dev and per_y == 1 and classes == 3 and nz_dev == 2
    assert lanes == 128 and length == 64
    slabs = nx_dev // 2
    depth = lanes // 2
    far = int(ny_dev > 2)
    edge, edge_y = (-(-n * 2 * half // 16) * 16 for n in (2, 2 + far))
    main = 2 * half * stride
    rows, rows_up = main + edge, main + edge_y
    g, row, core = (lax.axis_index(n) for n in ("gx", "gy", "gz"))
    scal = jnp.stack([g, row, core]).astype(jnp.int32)
    dims = dict(
        length=length, half=half, stride=stride, slabs=slabs, rows=rows, edge=edge, far=far,
        rows_y=ny_dev, depth=depth, extent_x=positions * stride,
        lines=(stride - 1, 0) + (length - 1,) * far,
    )
    weights = jnp.asarray(z_weights(length, depth))

    def ship(array, axis, by):
        size = lax.axis_size(axis)
        pairs = [(i, i + by) for i in range(size) if 0 <= i + by < size]
        return lax.ppermute(array, axis, pairs)

    def upper(g, core):
        return ((g * 2 + core) * half >= stride).astype(jnp.int32)

    def swapped(first):
        def base(g, core):
            start = ((g ^ first) & ~(slabs - 1)) - upper(g, core)
            return jnp.clip(start, 0, positions - slabs)

        shape = (slabs, 1, 3, half, length, 128)
        (other,) = call(
            functools.partial(pick_kernel, dict(dims, count=slabs, base=base)), scal,
            [pltpu.with_memory_space_constraint(patches, pltpu.HBM) if first else patches],
            [pltpu.VMEM(shape, jnp.bfloat16)],
            in_specs=[pl.BlockSpec(memory_space=pl.ANY)],
            out_specs=[pl.BlockSpec(memory_space=pltpu.VMEM)],
            scratch=[pltpu.SemaphoreType.DMA(())],
        )
        return lax.ppermute(other, "gz", [(0, 1), (1, 0)]), base

    def messages(first, count, recv, base):
        d = dict(dims, first=first, count=count, base=base)
        own, up, ahead = call(
            functools.partial(fold_kernel, d), scal, [patches, recv, weights],
            [
                like((count, 2 * half, stride, 128)),
                like((count, rows_up, 128), jnp.bfloat16),
                like((count, 2 * half, 128)),
            ],
            scratch=[vmem(length, 128), vmem(edge_y, 128)],
        )
        if ny_dev == 2:
            below = above = lax.ppermute(up, "gy", [(0, 1), (1, 0)])
        else:
            below, above = ship(up, "gy", 1), ship(up, "gy", -1)
        beyond = [ship(up, "gy", 2)] * far
        parts = call(
            functools.partial(join_kernel, d), scal,
            [own, ahead, below, above] + beyond,
            [like((rows, 128), jnp.bfloat16)] * count,
        )
        return [
            lax.ppermute(p, "gx", [(i, i ^ s) for i in range(nx_dev)]) if s else p
            for s, p in enumerate(parts, first)
        ]

    recv_far = swapped(slabs)
    recv_near = swapped(0)
    first = messages(slabs, slabs // 2, *recv_far)
    second = messages(slabs + slabs // 2, slabs // 2, *recv_far)
    third = messages(0, slabs, *recv_near)
    codes = third + first + second

    half_rows = (slabs, half, stride, 128)
    (ends,) = call(
        functools.partial(edge_kernel, dims), scal, codes, [like((2, stride, 128))],
        scratch=[vmem(half, 2, stride + 16, 128)],
    )
    above = [(2 * i + 1, 2 * i + 3) for i in range(nx_dev - 1)]
    below = [(2 * i + 2, 2 * i) for i in range(nx_dev - 1)]
    mine = lax.ppermute(ends, ("gx", "gz"), above + below)
    codes, _ = lax.optimization_barrier((codes, ends))
    keep, send = call(
        functools.partial(smooth_kernel, dims), scal, codes, [like(half_rows)] * 2,
        scratch=[vmem(slabs, half, 2, stride + 16, 128)],
    )
    recv = lax.ppermute(send, "gz", [(0, 1), (1, 0)])
    theirs = lax.ppermute(mine, "gz", [(0, 1), (1, 0)])

    step = slabs // 2
    return tuple(
        call(
            functools.partial(finish_kernel, dict(dims, step=step)), scal,
            [keep, recv, mine, theirs],
            [like((3, stride, stride, depth)), like((stride, stride, depth))],
            out_specs=[
                pl.BlockSpec((3, 2 * half * step, stride, depth), lambda i, s: (0, i, 0, 0)),
                pl.BlockSpec((2 * half * step, stride, depth), lambda i, s: (i, 0, 0)),
            ],
            grid=(slabs // step,),
            mib=8,
        )
    )


def solution(mesh):
    in_specs = (P(None, "gy", None, "gx", None, "gz"),)
    out_specs = (P(None, "gx", "gy", "gz"), P("gx", "gy", "gz"))
    return jax.shard_map(
        stitched, mesh=mesh, in_specs=in_specs, out_specs=out_specs, check_vma=False
    )
```

```python
import functools
import math

import jax
import jax.numpy as jnp
import numpy as np
from jax import lax
from jax.experimental import pallas as pl
from jax.experimental.pallas import tpu as pltpu
from jax.sharding import PartitionSpec as P


KNEE = 2.0
BASE = 2.0 ** (-120 / 33)
POWER = 33
LOG2E = 1.4426950408889634


def encode(d):
    t = d * (BASE / KNEE) + jnp.where(d < 0.0, -BASE, BASE)
    p = t
    for _ in range(5):
        p = p * p
    return (p * t).astype(jnp.bfloat16)


def decode(code, scale=1.0):
    v = code.astype(jnp.float32)
    t = jnp.exp2(jnp.log(jnp.abs(v)) * (LOG2E / POWER))
    k = scale * (KNEE / BASE)
    return (t - BASE) * jnp.where(v < 0.0, -k, k)


def share(cell, length, paired):
    stride = length // 2
    centre, spread = (length - 1) / 2.0, length / 8.0
    other = jnp.where(cell < stride, cell + stride, cell - stride).astype(jnp.float32)
    mine = cell.astype(jnp.float32)
    ratio = ((mine - centre) ** 2 - (other - centre) ** 2) / (2.0 * spread * spread)
    alone = jnp.logical_and(cell < stride, jnp.logical_not(paired))
    return jnp.where(alone, 1.0, 1.0 / (1.0 + jnp.exp(ratio)))


def z_weights(length, depth):
    stride, count = length // 2, 2 * depth // (length // 2)
    u = np.arange(length, dtype=np.float64)
    g = np.exp(-((u - (length - 1) / 2.0) ** 2) / (2.0 * (length / 8.0) ** 2))
    table = np.zeros((count * length, 2 * depth), np.float32)
    for k in range(count):
        for w in range(length):
            z = k * stride + w
            if z < 2 * depth:
                alone = k == 0 and w < stride
                pair = 0.0 if alone else g[w + stride if w < stride else w - stride]
                table[k * length + w, z] = g[w] / (g[w] + pair)
    high = table.astype(jnp.bfloat16)
    low = (table - high.astype(np.float32)).astype(jnp.bfloat16)
    both = np.concatenate([high, low], 1)
    return np.stack([both, np.roll(both, count * length // 2, 0)])


def place():
    return tuple(lax.axis_index(name) for name in ("gx", "gy", "gz"))


def index(shape, axis):
    return lax.broadcasted_iota(jnp.int32, shape, axis)


def pick_kernel(dims, patches, out, sem):
    scal = place()
    count, half = dims["count"], dims["half"]
    start = dims["base"](scal[0], scal[2])
    rows = pl.ds((1 - scal[2]) * half, half)
    copy = pltpu.make_async_copy(patches.at[pl.ds(start, count), :, :, rows], out, sem)
    copy.start()
    copy.wait()


def fold_kernel(dims, own_ref, recv_ref, w_ref, own_out, up_out, next_out, ny, edge):
    scal = place()
    length, half, stride, first = dims["length"], dims["half"], dims["stride"], dims["first"]
    g, row, core = scal[0], scal[1], scal[2]
    begin = (g * 2 + core) * half
    upper = (begin >= stride).astype(jnp.int32)
    cell = index((length, 128), 0)
    ny[...] = share(cell, length, jnp.full(cell.shape, row) > 0)
    edge[...] = jnp.zeros_like(edge)
    shape = (8, 128)
    nx_pair = [
        share(jnp.full(shape, begin + u), length, jnp.full(shape, 1) > 0) for u in range(half)
    ]
    weights = w_ref[core]

    def body(i, carry):
        a = (g ^ (first + i)) - upper
        at = jnp.maximum(a, 0)
        recv_at = at - dims["base"](g, core)
        for u in range(half):
            nx = jnp.where(jnp.logical_and(a == 0, upper == 0), 1.0, nx_pair[u])
            nx = jnp.where(a < 0, 0.0, nx)
            both = (ny[...].reshape(-1, 8, 128) * nx).reshape(length, 128)
            rows = [
                jnp.concatenate([own_ref[at, 0, k, core * half + u], recv_ref[recv_at, 0, k, u]], 1)
                for k in range(3)
            ]
            part = jnp.dot(
                jnp.concatenate(rows, 0), weights, preferred_element_type=jnp.float32
            )
            part = part[:, :128] + part[:, 128:]
            for k in range(2):
                total = (part[(k + 1) * length : (k + 2) * length] - part[:length]) * both
                j = k * half + u
                own_out[i, j] = total[:stride]
                up_out[i, j * stride : (j + 1) * stride] = encode(total[stride:])
                for n, line in enumerate(dims["lines"]):
                    edge[2 * half * n + j : 2 * half * n + j + 1] = total[line : line + 1]
                next_out[i, j : j + 1] = total[stride : stride + 1]
        up_out[i, 2 * half * stride :] = encode(edge[...])
        return carry

    lax.fori_loop(0, dims["count"], body, 0, unroll=2)


def join_kernel(dims, own_ref, next_ref, up_ref, down_ref, *refs):
    scal = place()
    half, stride, count, edge_rows = dims["half"], dims["stride"], dims["count"], dims["edge"]
    far = refs[:-count]
    outs = refs[len(far) : len(far) + count]
    row, rows_y = scal[1], dims["rows_y"]
    from_below = (row > 0).astype(jnp.float32)
    from_above = (row < rows_y - 1).astype(jnp.float32)
    main, group = 2 * half * stride, 2 * half

    def body(j, carry):
        part = pl.ds(pl.multiple_of(j * stride, stride), stride)
        for k in range(count):
            outs[k][part] = encode(own_ref[k, j] + decode(up_ref[k, part], from_below))
        return carry

    lax.fori_loop(0, 2 * half, body, 0, unroll=4)
    for k in range(count):
        lo = decode(up_ref[k, main:], from_below)[:group]
        hi = next_ref[k] + decode(down_ref[k, main:], from_above)[group : 2 * group]
        for f in far:
            beyond = (row > 1).astype(jnp.float32)
            lo += decode(f[k, main:], beyond)[2 * group : 3 * group]
        both = jnp.concatenate([lo, hi], axis=0)
        if edge_rows > 2 * group:
            both = jnp.concatenate([both] * (edge_rows // (2 * group)), axis=0)
        outs[k][main:] = encode(both)


def z_sum(p):
    lanes = index(p.shape, p.ndim - 1)
    before = jnp.where(lanes == 0, 0.0, pltpu.roll(p, 1, p.ndim - 1))
    after = jnp.where(lanes == 127, 0.0, pltpu.roll(p, 127, p.ndim - 1))
    return before + p + after


def two_classes(d1, d2):
    top = jnp.maximum(jnp.maximum(d1, d2), 0.0)
    e0, e1, e2 = jnp.exp2(-top), jnp.exp2(d1 - top), jnp.exp2(d2 - top)
    inverse = 1.0 / (e0 + e1 + e2)
    return e0 * inverse, e1 * inverse


def ends_of(dims, scal, here, there, pad):
    half, stride = dims["half"], dims["stride"]
    main = slice(2 * half * stride, None)
    d = decode(here[main], LOG2E) + decode(there[main], LOG2E)
    row = scal[1]
    for k, p in enumerate(two_classes(d, jnp.concatenate([d[half:], d[:half]], axis=0))):
        for u in range(half):
            lo, hi = p[u : u + 1], p[2 * half + u : 2 * half + u + 1]
            pad[u, k, 7:8] = jnp.where(row > 0, lo, 0.0)
            pad[u, k, 8 + stride : 9 + stride] = jnp.where(row < dims["rows_y"] - 1, hi, 0.0)


def halves_of(dims, here, there, u, pad):
    half, stride = dims["half"], dims["stride"]

    def total(j):
        part = pl.ds(pl.multiple_of(j * stride, stride), stride)
        return decode(here[part], LOG2E) + decode(there[part], LOG2E)

    sums = []
    for k, p in enumerate(two_classes(total(u), total(half + u))):
        at = pad.at[u, k]
        at[8 : 8 + stride] = p
        sums.append(z_sum(at[7 : 7 + stride] + p + at[9 : 9 + stride]))
    left = index((stride, 128), 1) < 64
    return (
        jnp.where(left, sums[0], pltpu.roll(sums[1], 64, 1)),
        jnp.where(left, pltpu.roll(sums[0], 64, 1), sums[1]),
    )


def edge_kernel(dims, *refs):
    scal = place()
    half, slabs = dims["half"], dims["slabs"]
    codes, ends, pad = refs[: 2 * slabs], refs[-2], refs[-1]
    g, core = scal[0], scal[2]
    low = core == 0
    at = (g & (slabs - 1)) ^ jnp.where(low, 0, slabs - 1)
    u = jnp.where(low, 0, half - 1)
    for s in range(slabs):

        @pl.when(at == s)
        def _():
            ends_of(dims, scal, codes[s], codes[s + slabs], pad)
            z0, z1 = halves_of(dims, codes[s], codes[s + slabs], u, pad)
            ends[0] = z0
            ends[1] = z1


def smooth_kernel(dims, *refs):
    scal = place()
    half, slabs = dims["half"], dims["slabs"]
    codes, keep, send, pad = refs[: 2 * slabs], refs[-3], refs[-2], refs[-1]
    g, core = scal[0], scal[2]
    low = core == 0
    for s in range(slabs):
        t = (g & (slabs - 1)) ^ s
        mine = pad.at[s]
        ends_of(dims, scal, codes[s], codes[s + slabs], mine)
        for u in range(half):
            z0, z1 = halves_of(dims, codes[s], codes[s + slabs], u, mine)
            keep[t, u] = jnp.where(low, z0, z1)
            send[t, u] = jnp.where(low, z1, z0)


def finish_kernel(dims, keep, recv, mine, theirs, smooth, confidence):
    scal = place()
    half, stride, slabs, depth = dims["half"], dims["stride"], dims["slabs"], dims["depth"]
    step = dims["step"]
    g, row, core = scal[0], scal[1], scal[2]
    low = core == 0
    t = pl.program_id(0) * step

    def lower(at, u):
        return jnp.where(low, keep[at, u], recv[at, u])

    def higher(at, u):
        return jnp.where(low, recv[at, u], keep[at, u])

    first = jnp.where(low, theirs[core], mine[core])
    last = jnp.where(low, mine[core], theirs[core])
    lines = [jnp.where(t > 0, higher(jnp.maximum(t - 1, 0), half - 1), first)]
    for i in range(step):
        lines += [lower(t + i, u) for u in range(half)]
        lines += [higher(t + i, u) for u in range(half)]
    end = t + step
    lines += [jnp.where(end < slabs, lower(jnp.minimum(end, slabs - 1), 0), last)]
    shape = (stride, 128)
    y = row * stride + index(shape, 0)
    z = core * depth + (index(shape, 1) & (depth - 1))

    def line_count(cell, extent):
        return 3.0 - (cell == 0).astype(jnp.float32) - (cell == extent - 1).astype(jnp.float32)

    inverse = 1.0 / (line_count(y, dims["rows_y"] * stride) * line_count(z, 2 * depth))
    for i in range(2 * half * step):
        x = jnp.full((8, 128), g * stride + t * 2 * half + i)
        scale = 1.0 / line_count(x, dims["extent_x"])
        total = (lines[i] + lines[i + 1] + lines[i + 2]) * inverse
        total = (total.reshape(-1, 8, 128) * scale).reshape(shape)
        c0 = total[:, :depth]
        c1 = pltpu.roll(total, 64, 1)[:, :depth]
        c2 = jnp.maximum(1.0 - (c0 + c1), 0.0)
        smooth[0, i] = c0
        smooth[1, i] = c1
        smooth[2, i] = c2
        confidence[i] = jnp.maximum(jnp.maximum(c0, c1), c2)


def vmem(*shape):
    return pltpu.VMEM(shape, jnp.float32)


def whole(shape):
    return pl.BlockSpec(shape, lambda *_: (0,) * len(shape))


def like(shape, dtype=jnp.float32):
    return jax.ShapeDtypeStruct(shape, dtype)


def call(kernel, args, outs, in_specs=None, out_specs=None, grid=(1,), scratch=(),
         mib=4, flops=0):
    args = list(args)
    size = sum(math.prod(a.shape) * a.dtype.itemsize for a in args + list(outs))
    return pl.pallas_call(
        kernel,
        out_shape=list(outs),
        grid=grid,
        in_specs=in_specs or [whole(a.shape) for a in args],
        out_specs=out_specs or [whole(o.shape) for o in outs],
        scratch_shapes=list(scratch),
        compiler_params=pltpu.CompilerParams(vmem_limit_bytes=int(mib * 2**20)),
        cost_estimate=pl.CostEstimate(flops=flops, bytes_accessed=size, transcendentals=0),
    )(*args)


def stitched(patches):
    positions, per_y, classes, slab, length, lanes = patches.shape
    nx_dev, ny_dev, nz_dev = (lax.axis_size(n) for n in ("gx", "gy", "gz"))
    stride = length // 2
    half = slab // nz_dev
    assert positions == nx_dev and per_y == 1 and classes == 3 and nz_dev == 2
    assert lanes == 128 and length == 64
    slabs = nx_dev // 2
    depth = lanes // 2
    far = int(ny_dev > 2)
    edge, edge_y = (-(-n * 2 * half // 16) * 16 for n in (2, 2 + far))
    main = 2 * half * stride
    rows, rows_up = main + edge, main + edge_y
    dims = dict(
        length=length, half=half, stride=stride, slabs=slabs, rows=rows, edge=edge, far=far,
        rows_y=ny_dev, depth=depth, extent_x=positions * stride,
        lines=(stride - 1, 0) + (length - 1,) * far,
    )
    weights = jnp.asarray(z_weights(length, depth))

    def ship(array, axis, by):
        size = lax.axis_size(axis)
        pairs = [(i, i + by) for i in range(size) if 0 <= i + by < size]
        return lax.ppermute(array, axis, pairs)

    def upper(g, core):
        return ((g * 2 + core) * half >= stride).astype(jnp.int32)

    def swapped(first):
        def base(g, core):
            start = ((g ^ first) & ~(slabs - 1)) - upper(g, core)
            return jnp.clip(start, 0, positions - slabs)

        shape = (slabs, 1, 3, half, length, 128)
        (other,) = call(
            functools.partial(pick_kernel, dict(dims, count=slabs, base=base)),
            [pltpu.with_memory_space_constraint(patches, pltpu.HBM) if first else patches],
            [pltpu.VMEM(shape, jnp.bfloat16)],
            in_specs=[pl.BlockSpec(memory_space=pl.ANY)],
            out_specs=[pl.BlockSpec(memory_space=pltpu.VMEM)],
            scratch=[pltpu.SemaphoreType.DMA(())],
        )
        return lax.ppermute(other, "gz", [(0, 1), (1, 0)]), base

    def messages(first, count, recv, base):
        d = dict(dims, first=first, count=count, base=base)
        own, up, ahead = call(
            functools.partial(fold_kernel, d), [patches, recv, weights],
            [
                like((count, 2 * half, stride, 128)),
                like((count, rows_up, 128), jnp.bfloat16),
                like((count, 2 * half, 128)),
            ],
            scratch=[vmem(length, 128), vmem(edge_y, 128)],
        )
        if ny_dev == 2:
            below = above = lax.ppermute(up, "gy", [(0, 1), (1, 0)])
        else:
            below, above = ship(up, "gy", 1), ship(up, "gy", -1)
        beyond = [ship(up, "gy", 2)] * far
        parts = call(
            functools.partial(join_kernel, d),
            [own, ahead, below, above] + beyond,
            [like((rows, 128), jnp.bfloat16)] * count,
        )
        return [
            lax.ppermute(p, "gx", [(i, i ^ s) for i in range(nx_dev)]) if s else p
            for s, p in enumerate(parts, first)
        ]

    recv_far = swapped(slabs)
    recv_near = swapped(0)
    first = messages(slabs, slabs // 2, *recv_far)
    second = messages(slabs + slabs // 2, slabs // 2, *recv_far)
    third = messages(1, slabs - 1, *recv_near)
    third = messages(0, 1, *recv_near) + third
    codes = third + first + second

    half_rows = (slabs, half, stride, 128)
    (ends,) = call(
        functools.partial(edge_kernel, dims), codes, [like((2, stride, 128))],
        scratch=[vmem(half, 2, stride + 16, 128)],
    )
    above = [(2 * i + 1, 2 * i + 3) for i in range(nx_dev - 1)]
    below = [(2 * i + 2, 2 * i) for i in range(nx_dev - 1)]
    mine = lax.ppermute(ends, ("gx", "gz"), above + below)
    codes, _ = lax.optimization_barrier((codes, ends))
    keep, send = call(
        functools.partial(smooth_kernel, dims), codes, [like(half_rows)] * 2,
        scratch=[vmem(slabs, half, 2, stride + 16, 128)],
    )
    recv = lax.ppermute(send, "gz", [(0, 1), (1, 0)])
    theirs = lax.ppermute(mine, "gz", [(0, 1), (1, 0)])

    step = slabs // 2
    return tuple(
        call(
            functools.partial(finish_kernel, dict(dims, step=step)),
            [keep, recv, mine, theirs],
            [like((3, stride, stride, depth)), like((stride, stride, depth))],
            out_specs=[
                pl.BlockSpec((3, 2 * half * step, stride, depth), lambda i: (0, i, 0, 0)),
                pl.BlockSpec((2 * half * step, stride, depth), lambda i: (i, 0, 0)),
            ],
            grid=(slabs // step,),
            mib=8,
        )
    )


def solution(mesh):
    in_specs = (P(None, "gy", None, "gx", None, "gz"),)
    out_specs = (P(None, "gx", "gy", "gz"), P("gx", "gy", "gz"))
    return jax.shard_map(
        stitched, mesh=mesh, in_specs=in_specs, out_specs=out_specs, check_vma=False
    )
```

```python
import functools
import math

import jax
import jax.numpy as jnp
import numpy as np
from jax import lax
from jax.experimental import pallas as pl
from jax.experimental.pallas import tpu as pltpu
from jax.sharding import PartitionSpec as P


KNEE = 2.0
BASE = 2.0 ** (-120 / 33)
POWER = 33
LOG2E = 1.4426950408889634


def encode(d):
    t = d * (BASE / KNEE) + jnp.where(d < 0.0, -BASE, BASE)
    p = t
    for _ in range(5):
        p = p * p
    return (p * t).astype(jnp.bfloat16)


def decode(code, scale=1.0):
    v = code.astype(jnp.float32)
    t = jnp.exp2(jnp.log(jnp.abs(v)) * (LOG2E / POWER))
    k = scale * (KNEE / BASE)
    return (t - BASE) * jnp.where(v < 0.0, -k, k)


def share(cell, length, paired):
    stride = length // 2
    centre, spread = (length - 1) / 2.0, length / 8.0
    other = jnp.where(cell < stride, cell + stride, cell - stride).astype(jnp.float32)
    mine = cell.astype(jnp.float32)
    ratio = ((mine - centre) ** 2 - (other - centre) ** 2) / (2.0 * spread * spread)
    alone = jnp.logical_and(cell < stride, jnp.logical_not(paired))
    return jnp.where(alone, 1.0, 1.0 / (1.0 + jnp.exp(ratio)))


def z_weights(length, depth):
    stride, count = length // 2, 2 * depth // (length // 2)
    u = np.arange(length, dtype=np.float64)
    g = np.exp(-((u - (length - 1) / 2.0) ** 2) / (2.0 * (length / 8.0) ** 2))
    table = np.zeros((count * length, 2 * depth), np.float32)
    for k in range(count):
        for w in range(length):
            z = k * stride + w
            if z < 2 * depth:
                alone = k == 0 and w < stride
                pair = 0.0 if alone else g[w + stride if w < stride else w - stride]
                table[k * length + w, z] = g[w] / (g[w] + pair)
    high = table.astype(jnp.bfloat16)
    low = (table - high.astype(np.float32)).astype(jnp.bfloat16)
    both = np.concatenate([high, low], 1)
    return np.stack([both, np.roll(both, count * length // 2, 0)])


def place():
    return tuple(lax.axis_index(name) for name in ("gx", "gy", "gz"))


def index(shape, axis):
    return lax.broadcasted_iota(jnp.int32, shape, axis)


def pick_kernel(dims, patches, out, sem):
    scal = place()
    count, half = dims["count"], dims["half"]
    start = dims["base"](scal[0], scal[2])
    rows = pl.ds((1 - scal[2]) * half, half)
    copy = pltpu.make_async_copy(patches.at[pl.ds(start, count), :, :, rows], out, sem)
    copy.start()
    copy.wait()


def fold_kernel(dims, own_ref, recv_ref, w_ref, own_out, up_out, next_out, ny, edge):
    scal = place()
    length, half, stride, first = dims["length"], dims["half"], dims["stride"], dims["first"]
    g, row, core = scal[0], scal[1], scal[2]
    begin = (g * 2 + core) * half
    upper = (begin >= stride).astype(jnp.int32)
    cell = index((length, 128), 0)
    ny[...] = share(cell, length, jnp.full(cell.shape, row) > 0)
    edge[...] = jnp.zeros_like(edge)
    shape = (8, 128)
    nx_pair = [
        share(jnp.full(shape, begin + u), length, jnp.full(shape, 1) > 0) for u in range(half)
    ]
    weights = w_ref[core]

    def body(i, carry):
        a = (g ^ (first + i)) - upper
        at = jnp.maximum(a, 0)
        recv_at = at - dims["base"](g, core)
        for u in range(half):
            nx = jnp.where(jnp.logical_and(a == 0, upper == 0), 1.0, nx_pair[u])
            nx = jnp.where(a < 0, 0.0, nx)
            both = (ny[...].reshape(-1, 8, 128) * nx).reshape(length, 128)
            rows = [
                jnp.concatenate([own_ref[at, 0, k, core * half + u], recv_ref[recv_at, 0, k, u]], 1)
                for k in range(3)
            ]
            part = jnp.dot(
                jnp.concatenate(rows, 0), weights, preferred_element_type=jnp.float32
            )
            part = part[:, :128] + part[:, 128:]
            for k in range(2):
                total = (part[(k + 1) * length : (k + 2) * length] - part[:length]) * both
                j = k * half + u
                own_out[i, j] = total[:stride]
                up_out[i, j * stride : (j + 1) * stride] = encode(total[stride:])
                for n, line in enumerate(dims["lines"]):
                    edge[2 * half * n + j : 2 * half * n + j + 1] = total[line : line + 1]
                next_out[i, j : j + 1] = total[stride : stride + 1]
        up_out[i, 2 * half * stride :] = encode(edge[...])
        return carry

    lax.fori_loop(0, dims["count"], body, 0, unroll=dims["count"] if dims["count"] < 4 else 2)


def join_kernel(dims, own_ref, next_ref, up_ref, down_ref, *refs):
    scal = place()
    half, stride, count, edge_rows = dims["half"], dims["stride"], dims["count"], dims["edge"]
    far = refs[:-count]
    outs = refs[len(far) : len(far) + count]
    row, rows_y = scal[1], dims["rows_y"]
    from_below = (row > 0).astype(jnp.float32)
    from_above = (row < rows_y - 1).astype(jnp.float32)
    main, group = 2 * half * stride, 2 * half

    def body(j, carry):
        part = pl.ds(pl.multiple_of(j * stride, stride), stride)
        for k in range(count):
            outs[k][part] = encode(own_ref[k, j] + decode(up_ref[k, part], from_below))
        return carry

    lax.fori_loop(0, 2 * half, body, 0, unroll=2 * half)
    for k in range(count):
        lo = decode(up_ref[k, main:], from_below)[:group]
        hi = next_ref[k] + decode(down_ref[k, main:], from_above)[group : 2 * group]
        for f in far:
            beyond = (row > 1).astype(jnp.float32)
            lo += decode(f[k, main:], beyond)[2 * group : 3 * group]
        both = jnp.concatenate([lo, hi], axis=0)
        if edge_rows > 2 * group:
            both = jnp.concatenate([both] * (edge_rows // (2 * group)), axis=0)
        outs[k][main:] = encode(both)


def z_sum(p):
    lanes = index(p.shape, p.ndim - 1)
    before = jnp.where(lanes == 0, 0.0, pltpu.roll(p, 1, p.ndim - 1))
    after = jnp.where(lanes == 127, 0.0, pltpu.roll(p, 127, p.ndim - 1))
    return before + p + after


def two_classes(d1, d2):
    top = jnp.maximum(jnp.maximum(d1, d2), 0.0)
    e0, e1, e2 = jnp.exp2(-top), jnp.exp2(d1 - top), jnp.exp2(d2 - top)
    inverse = 1.0 / (e0 + e1 + e2)
    return e0 * inverse, e1 * inverse


def ends_of(dims, scal, here, there, pad):
    half, stride = dims["half"], dims["stride"]
    main = slice(2 * half * stride, None)
    d = decode(here[main], LOG2E) + decode(there[main], LOG2E)
    row = scal[1]
    for k, p in enumerate(two_classes(d, jnp.concatenate([d[half:], d[:half]], axis=0))):
        for u in range(half):
            lo, hi = p[u : u + 1], p[2 * half + u : 2 * half + u + 1]
            pad[u, k, 7:8] = jnp.where(row > 0, lo, 0.0)
            pad[u, k, 8 + stride : 9 + stride] = jnp.where(row < dims["rows_y"] - 1, hi, 0.0)


def halves_of(dims, here, there, u, pad):
    half, stride = dims["half"], dims["stride"]

    def total(j):
        part = pl.ds(pl.multiple_of(j * stride, stride), stride)
        return decode(here[part], LOG2E) + decode(there[part], LOG2E)

    sums = []
    for k, p in enumerate(two_classes(total(u), total(half + u))):
        at = pad.at[u, k]
        at[8 : 8 + stride] = p
        sums.append(z_sum(at[7 : 7 + stride] + p + at[9 : 9 + stride]))
    left = index((stride, 128), 1) < 64
    return (
        jnp.where(left, sums[0], pltpu.roll(sums[1], 64, 1)),
        jnp.where(left, pltpu.roll(sums[0], 64, 1), sums[1]),
    )


def edge_kernel(dims, *refs):
    scal = place()
    half, slabs = dims["half"], dims["slabs"]
    codes, ends, pad = refs[: 2 * slabs], refs[-2], refs[-1]
    g, core = scal[0], scal[2]
    low = core == 0
    at = (g & (slabs - 1)) ^ jnp.where(low, 0, slabs - 1)
    u = jnp.where(low, 0, half - 1)
    for s in range(slabs):

        @pl.when(at == s)
        def _():
            ends_of(dims, scal, codes[s], codes[s + slabs], pad)
            z0, z1 = halves_of(dims, codes[s], codes[s + slabs], u, pad)
            ends[0] = z0
            ends[1] = z1


def smooth_kernel(dims, *refs):
    scal = place()
    half, slabs = dims["half"], dims["slabs"]
    codes, keep, send, pad = refs[: 2 * slabs], refs[-3], refs[-2], refs[-1]
    g, core = scal[0], scal[2]
    low = core == 0
    for s in range(slabs):
        t = (g & (slabs - 1)) ^ s
        mine = pad.at[s]
        ends_of(dims, scal, codes[s], codes[s + slabs], mine)
        for u in range(half):
            z0, z1 = halves_of(dims, codes[s], codes[s + slabs], u, mine)
            keep[t, u] = jnp.where(low, z0, z1)
            send[t, u] = jnp.where(low, z1, z0)


def line_count(cell, extent):
    return 3.0 - (cell == 0).astype(jnp.float32) - (cell == extent - 1).astype(jnp.float32)


class Rows:
    def __init__(self, dims, keep, recv):
        self.dims, self.keep, self.recv = dims, keep, recv
        stride, depth = dims["stride"], dims["depth"]
        self.g, row, core = place()
        self.low = core == 0
        self.shape = (stride, 128)
        y = row * stride + index(self.shape, 0)
        z = core * depth + (index(self.shape, 1) & (depth - 1))
        self.inverse = 1.0 / (line_count(y, dims["rows_y"] * stride) * line_count(z, 2 * depth))

    def lower(self, at, u):
        return jnp.where(self.low, self.keep[at, u], self.recv[at, u])

    def higher(self, at, u):
        return jnp.where(self.low, self.recv[at, u], self.keep[at, u])

    def results(self, before, here, after, x):
        depth = self.dims["depth"]
        cell = jnp.full((8, 128), self.g * self.dims["stride"] + x)
        scale = 1.0 / line_count(cell, self.dims["extent_x"])
        total = (before + here + after) * self.inverse
        total = (total.reshape(-1, 8, 128) * scale).reshape(self.shape)
        c0 = total[:, :depth]
        c1 = pltpu.roll(total, 64, 1)[:, :depth]
        c2 = jnp.maximum(1.0 - (c0 + c1), 0.0)
        return c0, c1, c2, jnp.maximum(jnp.maximum(c0, c1), c2)


def finish_kernel(dims, keep, recv, smooth, confidence):
    half, slabs, step = dims["half"], dims["slabs"], dims["step"]
    rows = Rows(dims, keep, recv)
    t = pl.program_id(0) * step
    end = t + step
    lines = [rows.higher(jnp.maximum(t - 1, 0), half - 1)]
    for i in range(step):
        lines += [rows.lower(t + i, u) for u in range(half)]
        lines += [rows.higher(t + i, u) for u in range(half)]
    lines += [rows.lower(jnp.minimum(end, slabs - 1), 0)]
    for i in range(2 * half * step):
        c0, c1, c2, top = rows.results(*lines[i : i + 3], t * 2 * half + i)
        smooth[0, i] = c0
        smooth[1, i] = c1
        smooth[2, i] = c2
        confidence[i] = top


def ends_kernel(dims, _, __, keep, recv, mine, theirs, smooth, confidence, parts, tops, sems):
    half, stride, slabs = dims["half"], dims["stride"], dims["slabs"]
    rows = Rows(dims, keep, recv)
    core = lax.axis_index("gz")
    first = jnp.where(rows.low, theirs[core], mine[core])
    last = jnp.where(rows.low, mine[core], theirs[core])
    end = slabs - 1
    triples = (
        (first, rows.lower(0, 0), rows.lower(0, 1)),
        (rows.higher(end, half - 2), rows.higher(end, half - 1), last),
    )
    copies = []
    for n, x in enumerate((0, stride - 1)):
        c0, c1, c2, top = rows.results(*triples[n], x)
        parts[0, n] = c0
        parts[1, n] = c1
        parts[2, n] = c2
        tops[n] = top
        copies += [
            pltpu.make_async_copy(parts.at[:, n], smooth.at[:, x], sems.at[2 * n]),
            pltpu.make_async_copy(tops.at[n], confidence.at[x], sems.at[2 * n + 1]),
        ]
    for copy in copies:
        copy.start()
    for copy in copies:
        copy.wait()


def vmem(*shape):
    return pltpu.VMEM(shape, jnp.float32)


def whole(shape):
    return pl.BlockSpec(shape, lambda *_: (0,) * len(shape))


def like(shape, dtype=jnp.float32):
    return jax.ShapeDtypeStruct(shape, dtype)


def call(kernel, args, outs, in_specs=None, out_specs=None, grid=(1,), scratch=(),
         mib=4, flops=0, aliases=None):
    args = list(args)
    size = sum(math.prod(a.shape) * a.dtype.itemsize for a in args + list(outs))
    return pl.pallas_call(
        kernel,
        out_shape=list(outs),
        grid=grid,
        in_specs=in_specs or [whole(a.shape) for a in args],
        out_specs=out_specs or [whole(o.shape) for o in outs],
        scratch_shapes=list(scratch),
        compiler_params=pltpu.CompilerParams(vmem_limit_bytes=int(mib * 2**20)),
        cost_estimate=pl.CostEstimate(flops=flops, bytes_accessed=size, transcendentals=0),
        input_output_aliases=aliases or {},
    )(*args)


def stitched(patches):
    positions, per_y, classes, slab, length, lanes = patches.shape
    nx_dev, ny_dev, nz_dev = (lax.axis_size(n) for n in ("gx", "gy", "gz"))
    stride = length // 2
    half = slab // nz_dev
    assert positions == nx_dev and per_y == 1 and classes == 3 and nz_dev == 2
    assert lanes == 128 and length == 64
    slabs = nx_dev // 2
    depth = lanes // 2
    far = int(ny_dev > 2)
    edge, edge_y = (-(-n * 2 * half // 16) * 16 for n in (2, 2 + far))
    main = 2 * half * stride
    rows, rows_up = main + edge, main + edge_y
    dims = dict(
        length=length, half=half, stride=stride, slabs=slabs, rows=rows, edge=edge, far=far,
        rows_y=ny_dev, depth=depth, extent_x=positions * stride,
        lines=(stride - 1, 0) + (length - 1,) * far,
    )
    weights = jnp.asarray(z_weights(length, depth))

    def ship(array, axis, by):
        size = lax.axis_size(axis)
        pairs = [(i, i + by) for i in range(size) if 0 <= i + by < size]
        return lax.ppermute(array, axis, pairs)

    def upper(g, core):
        return ((g * 2 + core) * half >= stride).astype(jnp.int32)

    def swapped(first):
        def base(g, core):
            start = ((g ^ first) & ~(slabs - 1)) - upper(g, core)
            return jnp.clip(start, 0, positions - slabs)

        shape = (slabs, 1, 3, half, length, 128)
        (other,) = call(
            functools.partial(pick_kernel, dict(dims, count=slabs, base=base)),
            [pltpu.with_memory_space_constraint(patches, pltpu.HBM) if first else patches],
            [pltpu.VMEM(shape, jnp.bfloat16)],
            in_specs=[pl.BlockSpec(memory_space=pl.ANY)],
            out_specs=[pl.BlockSpec(memory_space=pltpu.VMEM)],
            scratch=[pltpu.SemaphoreType.DMA(())],
        )
        return lax.ppermute(other, "gz", [(0, 1), (1, 0)]), base

    def messages(first, count, recv, base):
        d = dict(dims, first=first, count=count, base=base)
        own, up, ahead = call(
            functools.partial(fold_kernel, d), [patches, recv, weights],
            [
                like((count, 2 * half, stride, 128)),
                like((count, rows_up, 128), jnp.bfloat16),
                like((count, 2 * half, 128)),
            ],
            scratch=[vmem(length, 128), vmem(edge_y, 128)],
        )
        if ny_dev == 2:
            below = above = lax.ppermute(up, "gy", [(0, 1), (1, 0)])
        else:
            below, above = ship(up, "gy", 1), ship(up, "gy", -1)
        beyond = [ship(up, "gy", 2)] * far
        parts = call(
            functools.partial(join_kernel, d),
            [own, ahead, below, above] + beyond,
            [like((rows, 128), jnp.bfloat16)] * count,
        )
        return [
            lax.ppermute(p, "gx", [(i, i ^ s) for i in range(nx_dev)]) if s else p
            for s, p in enumerate(parts, first)
        ]

    recv_far = swapped(slabs)
    recv_near = swapped(0)
    first = messages(slabs, slabs // 2, *recv_far)
    second = messages(slabs + slabs // 2, slabs // 2, *recv_far)
    third = messages(1, slabs - 1, *recv_near)
    third = messages(0, 1, *recv_near) + third
    codes = third + first + second

    half_rows = (slabs, half, stride, 128)
    (ends,) = call(
        functools.partial(edge_kernel, dims), codes, [like((2, stride, 128))],
        scratch=[vmem(half, 2, stride + 16, 128)],
    )
    above = [(2 * i + 1, 2 * i + 3) for i in range(nx_dev - 1)]
    below = [(2 * i + 2, 2 * i) for i in range(nx_dev - 1)]
    mine = lax.ppermute(ends, ("gx", "gz"), above + below)
    codes, _ = lax.optimization_barrier((codes, ends))
    keep, send = call(
        functools.partial(smooth_kernel, dims), codes, [like(half_rows)] * 2,
        scratch=[vmem(slabs, half, 2, stride + 16, 128)],
    )
    recv = lax.ppermute(send, "gz", [(0, 1), (1, 0)])
    theirs = lax.ppermute(mine, "gz", [(0, 1), (1, 0)])

    step = slabs // 2
    outs = [like((3, stride, stride, depth)), like((stride, stride, depth))]
    inner = call(
        functools.partial(finish_kernel, dict(dims, step=step)), [keep, recv], outs,
        out_specs=[
            pl.BlockSpec((3, 2 * half * step, stride, depth), lambda i: (0, i, 0, 0)),
            pl.BlockSpec((2 * half * step, stride, depth), lambda i: (i, 0, 0)),
        ],
        grid=(slabs // step,),
        mib=8,
    )
    args = [keep, recv, mine, theirs]
    in_place = [pl.BlockSpec(memory_space=pl.ANY)] * 2
    return tuple(
        call(
            functools.partial(ends_kernel, dims), list(inner) + args, outs,
            in_specs=in_place + [whole(a.shape) for a in args],
            out_specs=in_place,
            scratch=[
                vmem(3, 2, stride, depth), vmem(2, stride, depth), pltpu.SemaphoreType.DMA((4,))
            ],
            aliases={0: 0, 1: 1},
        )
    )


def solution(mesh):
    in_specs = (P(None, "gy", None, "gx", None, "gz"),)
    out_specs = (P(None, "gx", "gy", "gz"), P("gx", "gy", "gz"))
    return jax.shard_map(
        stitched, mesh=mesh, in_specs=in_specs, out_specs=out_specs, check_vma=False
    )
```
